32 devices in a mesh: groups: 2 (over x), rows: 16 (over z, y, core).
Axes of the slice: x: 2, y: 2, z: 4, core: 2. Of those that a mesh axis runs over, the one named last changes fastest.
Arguments:
- features: bfloat16 [32768, 384], P(('groups', 'rows')), parts along dimension 0, may hold values from -8 to 8
- iterate: float32 [32768, 64], P(('groups', 'rows')), parts along dimension 0, may hold values from -6 to 6
- band_mask: int32 [32, 2], P(('groups', 'rows')), parts along dimension 0, may hold values from 0 to 1, as said below
Outputs:
- eigvecs: float32 [32768, 64], P(('groups', 'rows')), parts along dimension 0
- degrees: float32 [32768], P(('groups', 'rows')), parts along dimension 0
The draws below stay inside these ranges and needn't reach their ends.
There are 2 independent parts, one for each index of `groups`. The reference program is written for one: setup_inputs(seed, part) draws one part's arguments, and reference() takes and returns one part's arrays. A program takes and returns all parts, laid end to end along the dimension named above; each array names one. Nothing has to cross between parts.
Inputs may be any that keep to these rules, and one draw needn't show every extreme that they name: band_mask[i, o] is 0 wherever i + o + 1 >= 16, and 1 wherever i + o + 1 == 15.
All inputs are finite; a program needn't handle non-finite values.
Results may differ from the reference program's by a relative error of at most 0.0067.
Values may be sent and summed in bfloat16 or wider, within the bound.
A program may use at most 64 MiB of HBM per device.

```python
import jax
import jax.numpy as jnp
from jax import lax

C = 384
K = 64
W = 2
ITERS = 2
BLK = 1024
NBLK = 16
TOKENS = 16384


def draw_band_mask(key, part):
    values = jax.random.randint(key, (NBLK, W), 0, 3)
    block_index = jnp.arange(NBLK, dtype=jnp.int32)[:, None]
    offset = jnp.arange(W, dtype=jnp.int32)[None, :] + 1
    inside = block_index + offset < NBLK
    last_touch = block_index + offset == NBLK - 1
    return jnp.where(inside & ((values > 0) | last_touch), 1, 0).astype(jnp.int32)


def draw_features(key, part):
    spread_count = max(BLK // 512, 1)
    centre_key, choose_key, flip_key, weight_key, jitter_key = jax.random.split(jax.random.fold_in(key, 7), 5)
    centres = jax.random.normal(centre_key, (NBLK * spread_count + 2 * spread_count, C), jnp.float32)
    block_of = jnp.arange(TOKENS, dtype=jnp.int32) // BLK
    chosen = block_of * spread_count + jax.random.randint(choose_key, (TOKENS,), 0, 3 * spread_count)
    sign_flip = (2 * jax.random.randint(flip_key, (TOKENS,), 0, 2) - 1).astype(jnp.float32)
    weights = jax.random.uniform(weight_key, (TOKENS,), jnp.float32, 0.7, 0.97)
    jitter = jax.random.normal(jitter_key, (TOKENS, C), jnp.float32)
    remainder = jnp.sqrt(1.0 - weights * weights)
    values = (sign_flip * weights)[:, None] * centres[chosen] + remainder[:, None] * jitter
    return jnp.clip(values, -8.0, 8.0).astype(jnp.bfloat16)


def block_scale(own_key, extent, cuts, smallest, high):
    def one(axis_at, blocks):
        steps = jax.random.uniform(jax.random.fold_in(jax.random.fold_in(own_key, 6), axis_at), (blocks,), jnp.float32, smallest / len(cuts), high / len(cuts))
        return jnp.repeat(jnp.exp(steps), extent[axis_at] // blocks).reshape((-1,) + (1,) * (len(extent) - axis_at - 1))

    factor_of = one(*cuts[0])
    for cut in cuts[1:]:
        factor_of = factor_of * one(*cut)
    return factor_of


def noise(key, dims, scale, limit, shards=(), held_as=jnp.bfloat16):
    gain = block_scale(key, dims, shards, -0.22, 0.18) if shards else 1.0
    values = jax.random.normal(key, dims, jnp.float32) * scale * gain
    return jnp.minimum(jnp.maximum(values, -limit), limit).astype(held_as)


def setup_inputs(seed: int = 0, part: int = 0) -> dict:
    splits = jax.random.split(jax.random.key(seed), 4)
    part_keys = jax.random.split(jax.random.fold_in(splits[3], part), 4)
    features = draw_features(jax.random.fold_in(jax.random.fold_in(splits[3], part), 71), part)
    iterate = noise(part_keys[1], (TOKENS, K), 1.0, 6.0, ((0, 16),), jnp.float32)
    band_mask = draw_band_mask(jax.random.fold_in(jax.random.fold_in(splits[3], part), 71), part)
    return {"features": features, "iterate": iterate, "band_mask": band_mask}


def unit_rows(features):
    values = features.astype(jnp.float32)
    return (values * lax.rsqrt(lax.optimization_barrier(jnp.sum(values * values, axis=-1, keepdims=True)) + 1e-06)).astype(jnp.bfloat16)

def affinity(left, right):
    count = left.shape[0]
    step = min(512, count)
    pieces = []
    for start in range(0, count, step):
        scores = lax.dot_general(left[start:start + step].astype(jnp.float32), right.astype(jnp.float32), (((1,), (1,)), ((), ())), preferred_element_type=jnp.float32)
        pieces.append(jnp.exp(scores).astype(jnp.bfloat16))
    return jnp.concatenate(pieces, 0)

def spread(own, mirrored):
    total = own
    for offset in range(1, W + 1):
        moved = jnp.concatenate([jnp.zeros_like(mirrored[:offset, offset - 1]), mirrored[:NBLK - offset, offset - 1]], 0)
        total = total + moved
    return total

def reference(features, iterate, band_mask):
    unit = unit_rows(features)

    def form(index):
        left = lax.dynamic_slice_in_dim(unit, index * BLK, BLK, 0)
        tiles = [affinity(left, left)]
        for offset in range(1, W + 1):
            where = (jnp.minimum(index + offset, NBLK - 1) * BLK).astype(jnp.int32)
            right = lax.dynamic_slice_in_dim(unit, where, BLK, 0)
            keep = band_mask[index, offset - 1].astype(jnp.bfloat16)
            tiles.append(affinity(left, right) * keep)
        return jnp.stack(tiles)
    blocks = jnp.arange(NBLK, dtype=jnp.int32)
    tiles = lax.map(form, blocks)

    def degree_terms(index):
        tile_set = tiles[index]
        own = lax.optimization_barrier(jnp.sum(tile_set[0].astype(jnp.float32), axis=1))
        mirrored = []
        for offset in range(1, W + 1):
            own = own + lax.optimization_barrier(jnp.sum(tile_set[offset].astype(jnp.float32), axis=1))
            mirrored.append(lax.optimization_barrier(jnp.sum(tile_set[offset].astype(jnp.float32), axis=0)))
        return (own, jnp.stack(mirrored))
    own_deg, mirr_deg = lax.map(degree_terms, blocks)
    degrees = spread(own_deg, mirr_deg).reshape(TOKENS)
    scale = lax.rsqrt(degrees)[:, None]
    current = iterate
    for step in range(ITERS):
        scaled = (current * scale).astype(jnp.bfloat16)

        def product_terms(index):
            tile_set = tiles[index]
            own_vec = lax.dynamic_slice_in_dim(scaled, index * BLK, BLK, 0)
            rows_sum = jnp.dot(tile_set[0].astype(jnp.float32), own_vec.astype(jnp.float32), preferred_element_type=jnp.float32)
            mirrored = []
            for offset in range(1, W + 1):
                where = (jnp.minimum(index + offset, NBLK - 1) * BLK).astype(jnp.int32)
                partner = lax.dynamic_slice_in_dim(scaled, where, BLK, 0)
                rows_sum = rows_sum + jnp.dot(tile_set[offset].astype(jnp.float32), partner.astype(jnp.float32), preferred_element_type=jnp.float32)
                mirrored.append(lax.dot_general(tile_set[offset].astype(jnp.float32), own_vec.astype(jnp.float32), (((0,), (0,)), ((), ())), preferred_element_type=jnp.float32))
            return (rows_sum, jnp.stack(mirrored))
        own_terms, mirr_terms = lax.map(product_terms, blocks)
        image = spread(own_terms, mirr_terms).reshape(TOKENS, K)
        normed = image * scale
        gram = jnp.dot(normed.T.astype(jnp.float32), normed.astype(jnp.float32), precision=lax.Precision.HIGHEST, preferred_element_type=jnp.float32)
        lower = jnp.linalg.cholesky(gram)
        current = jax.scipy.linalg.solve_triangular(lower, normed.T, lower=True).T
    return (current, degrees)
```

```python
import functools

import jax
import jax.numpy as jnp
from jax import lax
from jax.experimental import pallas as pl
from jax.experimental.pallas import tpu as pltpu
from jax.sharding import PartitionSpec as P

W = 2
ITERS = 2
PARTS = 8
CUTS = 2
AXIS = "rows"
MESH = pl.DeviceIdType.MESH
HIGH = lax.Precision.HIGHEST


def radices(count):
    out = []
    while count > 1:
        radix = next((r for r in (4, 2, 3, 5, 7) if count % r == 0), count)
        out.append(radix)
        count //= radix
    return out


def peers_of(me, plan):
    stride = 1
    found = []
    for radix in plan:
        digit = lax.rem(lax.div(me, stride), radix)
        row = []
        for k in range(1, radix):
            other = lax.rem(digit + k, radix)
            row.append((other, me + (other - digit) * stride))
        found.append((digit, row))
        stride *= radix
    return found


def all_sum(value, found, box, send_sem, recv_sem):
    for phase, (digit, row) in enumerate(found):
        box[phase, digit] = value
        copies = []
        for k, (other, peer) in enumerate(row):
            copy = pltpu.make_async_remote_copy(
                src_ref=box.at[phase, digit],
                dst_ref=box.at[phase, digit],
                send_sem=send_sem.at[phase, k],
                recv_sem=recv_sem.at[phase, digit],
                device_id={AXIS: peer},
                device_id_type=MESH,
            )
            copy.start()
            copies.append(copy)
        for other, peer in row:
            pltpu.make_async_remote_copy(
                src_ref=box.at[phase, other],
                dst_ref=box.at[phase, other],
                send_sem=send_sem.at[phase, 0],
                recv_sem=recv_sem.at[phase, other],
                device_id={AXIS: peer},
                device_id_type=MESH,
            ).wait_recv()
        value = box[phase, 0]
        for slot in range(1, len(row) + 1):
            value = value + box[phase, slot]
        for copy in copies:
            copy.wait_send()
    return value


def inverse_factor(gram):
    size = gram.shape[0]
    rows = lax.broadcasted_iota(jnp.int32, (size, size), 0)
    cols = lax.broadcasted_iota(jnp.int32, (size, size), 1)
    both = jnp.concatenate([gram, jnp.where(rows == cols, 1.0, 0.0)], axis=1)
    count = size // 8
    bands = [both[8 * b : 8 * b + 8] for b in range(count)]
    sub = lax.broadcasted_iota(jnp.int32, (8, 1), 0)
    pivots = []
    for j in range(size):
        b, s = j // 8, j % 8
        row = bands[b][s : s + 1]
        pivot = row[:, j : j + 1]
        pivots.append(pivot)
        scaled = row * (1.0 / pivot)
        for c in range(b, count):
            column = bands[c][:, j : j + 1]
            if c == b:
                column = jnp.where(sub > s, column, 0.0)
            bands[c] = bands[c] - column * scaled
    out = []
    for b in range(count):
        diagonal = jnp.zeros((8, 1), jnp.float32)
        for s in range(8):
            diagonal = jnp.where(sub == s, pivots[8 * b + s], diagonal)
        out.append(bands[b][:, size:] * lax.rsqrt(diagonal))
    return jnp.concatenate(out, axis=0)


def pack(gram):
    half = gram.shape[0] // 2
    return jnp.concatenate([gram[:half], gram[half:]], axis=1)


def unpack(packed):
    size = packed.shape[1] // 2
    return jnp.concatenate([packed[:, :size], packed[:, size:]], axis=0)


OWN, PEER, ALONG, RELAYED, PASSED = range(5)
ROWS_CONTRACTED = (((1,), (0,)), ((), ()))
LAST_CONTRACTED = (((1,), (1,)), ((), ()))


def fused_kernel(plan, peers, parts, cuts, feature_ref, start_ref, mask_ref, *refs):
    out_ref, degree_ref = refs[:2]
    unit, tile, sums, keep, acc, normed, first, second, box = refs[2:11]
    u_out, u_in, k_out, k_in, p_out, p_in, send_sem, recv_sem = refs[11:]
    me = lax.axis_index(AXIS)
    core = lax.rem(me, 2)
    side = lax.rem(lax.div(me, 2), 2)
    role = core + side - 2 * core * side
    peer = me + 1 - 2 * core
    along = me + 2 - 4 * side
    ahead = me + 4 - 8 * side
    behind = me - 4 + 8 * side
    has_ahead = (ahead >= 0) & (ahead < peers)
    has_behind = (behind >= 0) & (behind < peers)
    has_passed = (role == 1) | has_behind
    found = peers_of(me, plan)

    row_at = lax.broadcasted_iota(jnp.int32, (8, 128), 0)
    flags = mask_ref[...].astype(jnp.float32)
    keep[0] = jnp.where(row_at == 0, flags[:, 0:1], jnp.where(row_at == 1, flags[:, 1:2], 0.0))
    keep[1] = jnp.zeros((8, 128), jnp.float32)
    keep[2] = jnp.zeros((8, 128), jnp.float32)

    barrier = pltpu.get_barrier_semaphore()
    total = 0
    for _, row in found:
        for _, other in row:
            pl.semaphore_signal(barrier, inc=1, device_id={AXIS: other}, device_id_type=MESH)
            total += 1
    for offset in (1, 2, 4):

        @pl.when(me >= offset)
        def _():
            pl.semaphore_signal(barrier, inc=1, device_id={AXIS: me - offset}, device_id_type=MESH)

        @pl.when(me + offset < peers)
        def _():
            pl.semaphore_signal(barrier, inc=1, device_id={AXIS: me + offset}, device_id_type=MESH)

        total = total + (me >= offset).astype(jnp.int32) + (me + offset < peers).astype(jnp.int32)

    size = feature_ref.shape[0]
    width = size // parts
    sums[...] = jnp.zeros_like(sums)

    def normalise(step, carry):
        at = pl.ds(pl.multiple_of(step * width, width), width)
        values = feature_ref[at].astype(jnp.float32)
        square = jnp.sum(values * values, axis=-1, keepdims=True)
        unit[OWN, at] = (values * lax.rsqrt(square + 1e-06)).astype(jnp.bfloat16)
        return carry

    lax.fori_loop(0, parts, normalise, 0)
    pl.semaphore_wait(barrier, total)

    def send(buffer, at, source, target, out_sem, in_sem, device):
        return pltpu.make_async_remote_copy(
            src_ref=buffer.at[(source,) + at],
            dst_ref=buffer.at[(target,) + at],
            send_sem=out_sem,
            recv_sem=in_sem,
            device_id={AXIS: device},
            device_id_type=MESH,
        )

    def unit_copy(target, step):
        at = (pl.ds(pl.multiple_of(step * width, width), width),)
        source, device = {
            PEER: (OWN, peer),
            ALONG: (OWN, along),
            RELAYED: (ALONG, ahead),
            PASSED: (ALONG + role, peer),
        }[target]
        sems = u_out.at[target, step], u_in.at[target, step]
        return send(unit, at, source, target, *sems, device)

    def keep_copy(offset):
        return send(keep, (), 0, offset, k_out.at[offset], k_in.at[offset], me + offset)

    def launch(step, carry):
        unit_copy(ALONG, step).start()
        unit_copy(PEER, step).start()
        return carry

    lax.fori_loop(0, parts, launch, 0)
    for offset in range(1, W + 1):

        @pl.when(me + offset < peers)
        def _():
            keep_copy(offset).start()

    def piece(slot, step):
        at = pl.ds(pl.multiple_of(step * width, width), width)
        scores = lax.dot_general(
            unit[slot, at], unit[OWN, :size], LAST_CONTRACTED, preferred_element_type=jnp.float32
        )
        values = jnp.exp(scores).astype(jnp.bfloat16)
        tile[slot, at] = values
        sums[slot] += jnp.sum(values.astype(jnp.float32).reshape(width // 8, 8, size), axis=0)

    def turn(step, carry):
        @pl.when(step < parts)
        def _():
            piece(OWN, step)
            unit_copy(PEER, step).wait_recv()
            piece(PEER, step)
            unit_copy(ALONG, step).wait_recv()

            @pl.when(has_ahead)
            def _():
                unit_copy(RELAYED, step).start()

            @pl.when(role == 0)
            def _():
                unit_copy(PASSED, step).start()

        late = (step >= 1) & (step <= parts) & has_behind

        @pl.when(late)
        def _():
            unit_copy(RELAYED, step - 1).wait_recv()

            @pl.when(role == 1)
            def _():
                unit_copy(PASSED, step - 1).start()

        @pl.when(step < parts)
        def _():
            piece(ALONG, step)

        @pl.when(late)
        def _():
            piece(RELAYED, step - 1)

        @pl.when((step >= 2) & has_passed)
        def _():
            unit_copy(PASSED, step - 2).wait_recv()
            piece(PASSED, step - 2)

        return carry

    lax.fori_loop(0, parts + 2, turn, 0)

    for offset in range(1, W + 1):

        @pl.when(me >= offset)
        def _():
            keep_copy(offset).wait_recv()

    up_one, up_two = keep[0][0:1], keep[0][1:2]
    down_one, down_two = keep[1][0:1], keep[2][1:2]
    chosen = {
        PEER: jnp.where(core == 0, up_one, down_one),
        ALONG: jnp.where(side == 0, up_two, down_two),
        RELAYED: jnp.where(side == 0, down_two, up_two),
        PASSED: jnp.where(core == 0, down_one, up_one),
    }
    spread = {slot: jnp.concatenate([row] * (size // 128), axis=1) for slot, row in chosen.items()}
    eight = sums[OWN]
    for slot in (PEER, ALONG, RELAYED, PASSED):
        eight = eight + spread[slot] * sums[slot]
    degrees = jnp.sum(eight, axis=0, keepdims=True)
    degree_ref[...] = degrees
    scale = lax.rsqrt(degrees)

    def block_copy(step, buffer, target, cut):
        length = size // cuts
        at = (slice(None), pl.ds(cut * length, length))
        source, device = {
            PEER: (OWN, peer),
            ALONG: (OWN, along),
            RELAYED: (ALONG, ahead),
            PASSED: (ALONG + role, peer),
        }[target]
        sems = p_out.at[step, target, cut], p_in.at[step, target, cut]
        return send(buffer, at, source, target, *sems, device)

    def begin(step, buffer):
        for cut in range(cuts):
            block_copy(step, buffer, ALONG, cut).start()
            block_copy(step, buffer, PEER, cut).start()

    def relay(step, buffer):
        for cut in range(cuts):
            block_copy(step, buffer, ALONG, cut).wait_recv()

            @pl.when(has_ahead)
            def _():
                block_copy(step, buffer, RELAYED, cut).start()

            @pl.when(role == 0)
            def _():
                block_copy(step, buffer, PASSED, cut).start()

    def relay_again(step, buffer):
        @pl.when(has_behind)
        def _():
            for cut in range(cuts):
                block_copy(step, buffer, RELAYED, cut).wait_recv()

                @pl.when(role == 1)
                def _():
                    block_copy(step, buffer, PASSED, cut).start()

    def product(buffer, slot):
        block = buffer[slot]
        if slot != OWN:
            block = block * spread[slot].astype(jnp.bfloat16)
        return lax.dot_general(block, tile[slot], ROWS_CONTRACTED, preferred_element_type=jnp.float32)

    def early(step, buffer):
        for cut in range(cuts):
            block_copy(step, buffer, PEER, cut).wait_recv()
        acc[: buffer.shape[1]] = product(buffer, OWN) + product(buffer, PEER)

    def late(step, buffer):
        count = buffer.shape[1]

        @pl.when(has_behind)
        def _():
            acc[:count] += product(buffer, RELAYED)

        @pl.when(has_passed)
        def _():
            for cut in range(cuts):
                block_copy(step, buffer, PASSED, cut).wait_recv()
            acc[:count] += product(buffer, PASSED)

    def gram_of(values):
        return lax.dot_general(
            values, values, LAST_CONTRACTED, precision=HIGH, preferred_element_type=jnp.float32
        )

    def total_of(step, gram):
        return unpack(all_sum(pack(gram), found, box.at[step], send_sem.at[step], recv_sem.at[step]))

    def applied(inverse, values):
        return lax.dot_general(
            inverse, values, ROWS_CONTRACTED, precision=HIGH, preferred_element_type=jnp.float32
        )

    first[OWN] = (start_ref[...] * scale).astype(jnp.bfloat16)
    begin(0, first)
    early(0, first)
    relay(0, first)
    acc[: first.shape[1]] += product(first, ALONG)
    relay_again(0, first)
    late(0, first)

    count = first.shape[1]
    normed[...] = acc[:count] * scale
    again = normed[...] * scale
    coarse = again.astype(jnp.bfloat16)
    second[OWN, :count] = coarse
    second[OWN, count:] = (again - coarse.astype(jnp.float32)).astype(jnp.bfloat16)
    begin(1, second)
    gram = total_of(0, gram_of(normed[...]))
    relay(1, second)
    early(1, second)
    acc[...] += product(second, ALONG)
    relay_again(1, second)
    inverse = inverse_factor(gram)
    late(1, second)
    image = (acc[:count] + acc[count:]) * scale
    normed[...] = applied(inverse, image)
    gram = total_of(1, gram_of(normed[...]))
    out_ref[...] = applied(inverse_factor(gram), normed[...])

    def settle(step, carry):
        unit_copy(ALONG, step).wait_send()
        unit_copy(PEER, step).wait_send()

        @pl.when(has_ahead)
        def _():
            unit_copy(RELAYED, step).wait_send()

        @pl.when((role == 0) | has_behind)
        def _():
            unit_copy(PASSED, step).wait_send()

        return carry

    lax.fori_loop(0, parts, settle, 0)
    for offset in range(1, W + 1):

        @pl.when(me + offset < peers)
        def _():
            keep_copy(offset).wait_send()

    for step, buffer in enumerate((first, second)):
        for cut in range(cuts):
            block_copy(step, buffer, ALONG, cut).wait_send()
            block_copy(step, buffer, PEER, cut).wait_send()

            @pl.when(has_ahead)
            def _():
                block_copy(step, buffer, RELAYED, cut).wait_send()

            @pl.when((role == 0) | has_behind)
            def _():
                block_copy(step, buffer, PASSED, cut).wait_send()


def local(peers, features, iterate, band_mask):
    size, depth = features.shape
    count = iterate.shape[1]
    plan = radices(peers)
    phases, widest = len(plan), max(plan)
    parts, cuts = PARTS, CUTS
    dma = pltpu.SemaphoreType.DMA
    current, degrees = pl.pallas_call(
        functools.partial(fused_kernel, plan, peers, parts, cuts),
        out_shape=(
            jax.ShapeDtypeStruct((count, size), jnp.float32),
            jax.ShapeDtypeStruct((1, size), jnp.float32),
        ),
        in_specs=[pl.BlockSpec(memory_space=pltpu.VMEM)] * 3,
        out_specs=(pl.BlockSpec(memory_space=pltpu.VMEM),) * 2,
        scratch_shapes=[
            pltpu.VMEM((5, size, depth), jnp.bfloat16),
            pltpu.VMEM((5, size, size), jnp.bfloat16),
            pltpu.VMEM((5, 8, size), jnp.float32),
            pltpu.VMEM((1 + W, 8, 128), jnp.float32),
            pltpu.VMEM((2 * count, size), jnp.float32),
            pltpu.VMEM((count, size), jnp.float32),
            pltpu.VMEM((5, count, size), jnp.bfloat16),
            pltpu.VMEM((5, 2 * count, size), jnp.bfloat16),
            pltpu.VMEM((ITERS, phases, widest, count // 2, 2 * count), jnp.float32),
            dma((5, parts)),
            dma((5, parts)),
            dma((1 + W,)),
            dma((1 + W,)),
            dma((ITERS, 5, cuts)),
            dma((ITERS, 5, cuts)),
            dma((ITERS, phases, widest)),
            dma((ITERS, phases, widest)),
        ],
        compiler_params=pltpu.CompilerParams(
            collective_id=0, has_side_effects=True, vmem_limit_bytes=48 << 20
        ),
        name="fused",
    )(features, iterate.T, band_mask)
    return (current.T, degrees[0])


def solution(mesh):
    return jax.shard_map(
        functools.partial(local, mesh.shape[AXIS]),
        mesh=mesh,
        in_specs=(
            P(("groups", "rows"), None),
            P(("groups", "rows"), None),
            P(("groups", "rows"), None),
        ),
        out_specs=(P(("groups", "rows"), None), P(("groups", "rows"))),
        check_vma=False,
    )
```

```python
import functools

import jax
import jax.numpy as jnp
from jax import lax
from jax.experimental import pallas as pl
from jax.experimental.pallas import tpu as pltpu
from jax.sharding import PartitionSpec as P

W = 2
ITERS = 2
PARTS = 8
CUTS = 4
AXIS = "rows"
MESH = pl.DeviceIdType.MESH
HIGH = lax.Precision.HIGHEST


def radices(count):
    out = []
    while count > 1:
        radix = next((r for r in (4, 2, 3, 5, 7) if count % r == 0), count)
        out.append(radix)
        count //= radix
    return out


def peers_of(me, plan):
    stride = 1
    found = []
    for radix in plan:
        digit = lax.rem(lax.div(me, stride), radix)
        row = []
        for k in range(1, radix):
            other = lax.rem(digit + k, radix)
            row.append((other, me + (other - digit) * stride))
        found.append((digit, row))
        stride *= radix
    return found


class Phase:
    def __init__(self, found, box, send_sem, recv_sem):
        self.digit, self.row = found
        self.box, self.send_sem, self.recv_sem = box, send_sem, recv_sem

    def copy(self, k, slot, peer):
        return pltpu.make_async_remote_copy(
            src_ref=self.box.at[slot],
            dst_ref=self.box.at[slot],
            send_sem=self.send_sem.at[k],
            recv_sem=self.recv_sem.at[slot],
            device_id={AXIS: peer},
            device_id_type=MESH,
        )

    def send(self, value):
        self.box[self.digit] = value
        for k, (_, peer) in enumerate(self.row):
            self.copy(k, self.digit, peer).start()

    def receive(self):
        for k, (other, peer) in enumerate(self.row):
            self.copy(k, other, peer).wait_recv()
        value = self.box[0]
        for slot in range(1, len(self.row) + 1):
            value = value + self.box[slot]
        return value

    def settle(self):
        for k, (_, peer) in enumerate(self.row):
            self.copy(k, self.digit, peer).wait_send()


def inverse_factor(gram, pauses):
    size = gram.shape[0]
    rows = lax.broadcasted_iota(jnp.int32, (size, size), 0)
    cols = lax.broadcasted_iota(jnp.int32, (size, size), 1)
    both = jnp.concatenate([gram, jnp.where(rows == cols, 1.0, 0.0)], axis=1)
    count = size // 8
    bands = [both[8 * b : 8 * b + 8] for b in range(count)]
    sub = lax.broadcasted_iota(jnp.int32, (8, 1), 0)
    pivots = []
    for j in range(size):
        if j in pauses:
            pauses[j]()
        b, s = j // 8, j % 8
        row = bands[b][s : s + 1]
        pivot = row[:, j : j + 1]
        pivots.append(pivot)
        scaled = row * (1.0 / pivot)
        for c in range(b, count):
            column = bands[c][:, j : j + 1]
            if c == b:
                column = jnp.where(sub > s, column, 0.0)
            bands[c] = bands[c] - column * scaled
    out = []
    for b in range(count):
        diagonal = jnp.zeros((8, 1), jnp.float32)
        for s in range(8):
            diagonal = jnp.where(sub == s, pivots[8 * b + s], diagonal)
        out.append(bands[b][:, size:] * lax.rsqrt(diagonal))
    return jnp.concatenate(out, axis=0)


def pack(gram):
    half = gram.shape[0] // 2
    return jnp.concatenate([gram[:half], gram[half:]], axis=1)


def unpack(packed):
    size = packed.shape[1] // 2
    return jnp.concatenate([packed[:, :size], packed[:, size:]], axis=0)


OWN, PEER, ALONG, RELAYED, PASSED = range(5)
ROWS_CONTRACTED = (((1,), (0,)), ((), ()))
LAST_CONTRACTED = (((1,), (1,)), ((), ()))


def fused_kernel(plan, peers, parts, cuts, feature_hbm, start_hbm, mask_hbm, *refs):
    out_ref, degree_ref = refs[:2]
    feature_ref, start_ref, mask_ref, unit, flipped, tile, sums, keep, acc, normed, first, second, box = refs[2:15]
    loads, u_out, u_in, k_out, k_in, p_out, p_in, send_sem, recv_sem = refs[15:]
    load_feature = pltpu.make_async_copy(feature_hbm, feature_ref, loads.at[0])
    load_mask = pltpu.make_async_copy(mask_hbm, mask_ref, loads.at[1])
    load_start = pltpu.make_async_copy(start_hbm, start_ref, loads.at[2])
    load_feature.start()
    load_mask.start()
    load_start.start()
    me = lax.axis_index(AXIS)
    core = lax.rem(me, 2)
    side = lax.rem(lax.div(me, 2), 2)
    role = core + side - 2 * core * side
    peer = me + 1 - 2 * core
    along = me + 2 - 4 * side
    ahead = me + 4 - 8 * side
    behind = me - 4 + 8 * side
    has_ahead = (ahead >= 0) & (ahead < peers)
    has_behind = (behind >= 0) & (behind < peers)
    has_passed = (role == 1) | has_behind
    found = peers_of(me, plan)

    keep[1] = jnp.zeros((8, 128), jnp.float32)
    keep[2] = jnp.zeros((8, 128), jnp.float32)

    barrier = pltpu.get_barrier_semaphore()
    total = 0
    for _, row in found:
        for _, other in row:
            pl.semaphore_signal(barrier, inc=1, device_id={AXIS: other}, device_id_type=MESH)
            total += 1
    for offset in (1, 2, 4):

        @pl.when(me >= offset)
        def _():
            pl.semaphore_signal(barrier, inc=1, device_id={AXIS: me - offset}, device_id_type=MESH)

        @pl.when(me + offset < peers)
        def _():
            pl.semaphore_signal(barrier, inc=1, device_id={AXIS: me + offset}, device_id_type=MESH)

        total = total + (me >= offset).astype(jnp.int32) + (me + offset < peers).astype(jnp.int32)

    size = feature_ref.shape[0]
    width = size // parts
    sums[...] = jnp.zeros_like(sums)
    load_feature.wait()

    def normalise(step, carry):
        at = pl.ds(pl.multiple_of(step * width, width), width)
        values = feature_ref[at].astype(jnp.float32)
        square = jnp.sum(values * values, axis=-1, keepdims=True)
        unit[OWN, at] = (values * lax.rsqrt(square + 1e-06)).astype(jnp.bfloat16)
        return carry

    lax.fori_loop(0, parts, normalise, 0)
    pl.semaphore_wait(barrier, total)

    def send(buffer, at, source, target, out_sem, in_sem, device):
        return pltpu.make_async_remote_copy(
            src_ref=buffer.at[(source,) + at],
            dst_ref=buffer.at[(target,) + at],
            send_sem=out_sem,
            recv_sem=in_sem,
            device_id={AXIS: device},
            device_id_type=MESH,
        )

    def unit_copy(target, step):
        at = (pl.ds(pl.multiple_of(step * width, width), width),)
        source, device = {
            PEER: (OWN, peer),
            ALONG: (OWN, along),
            RELAYED: (ALONG, ahead),
            PASSED: (ALONG + role, peer),
        }[target]
        sems = u_out.at[target, step], u_in.at[target, step]
        return send(unit, at, source, target, *sems, device)

    def keep_copy(offset):
        return send(keep, (), 0, offset, k_out.at[offset], k_in.at[offset], me + offset)

    def launch(step, carry):
        unit_copy(ALONG, step).start()
        unit_copy(PEER, step).start()
        return carry

    lax.fori_loop(0, parts, launch, 0)
    load_mask.wait()
    row_at = lax.broadcasted_iota(jnp.int32, (8, 128), 0)
    flags = mask_ref[...].astype(jnp.float32)
    keep[0] = jnp.where(row_at == 0, flags[:, 0:1], jnp.where(row_at == 1, flags[:, 1:2], 0.0))
    flipped[...] = unit[OWN].T
    for offset in range(1, W + 1):

        @pl.when(me + offset < peers)
        def _():
            keep_copy(offset).start()

    def piece(slot, step):
        at = pl.ds(pl.multiple_of(step * width, width), width)
        scores = lax.dot_general(
            unit[slot, at], flipped[...], ROWS_CONTRACTED, preferred_element_type=jnp.float32
        )
        values = jnp.exp(scores).astype(jnp.bfloat16)
        tile[slot, at] = values
        sums[slot] += jnp.sum(values.astype(jnp.float32).reshape(width // 8, 8, size), axis=0)

    def turn(step, carry):
        @pl.when(step < parts)
        def _():
            piece(OWN, step)
            unit_copy(PEER, step).wait_recv()
            piece(PEER, step)
            unit_copy(ALONG, step).wait_recv()

            @pl.when(has_ahead)
            def _():
                unit_copy(RELAYED, step).start()

            @pl.when(role == 0)
            def _():
                unit_copy(PASSED, step).start()

        late = (step >= 1) & (step <= parts) & has_behind

        @pl.when(late)
        def _():
            unit_copy(RELAYED, step - 1).wait_recv()

            @pl.when(role == 1)
            def _():
                unit_copy(PASSED, step - 1).start()

        @pl.when(step < parts)
        def _():
            piece(ALONG, step)

        @pl.when(late)
        def _():
            piece(RELAYED, step - 1)

        @pl.when((step >= 2) & has_passed)
        def _():
            unit_copy(PASSED, step - 2).wait_recv()
            piece(PASSED, step - 2)

        return carry

    lax.fori_loop(0, parts + 2, turn, 0)

    for offset in range(1, W + 1):

        @pl.when(me >= offset)
        def _():
            keep_copy(offset).wait_recv()

    up_one, up_two = keep[0][0:1], keep[0][1:2]
    down_one, down_two = keep[1][0:1], keep[2][1:2]
    chosen = {
        PEER: jnp.where(core == 0, up_one, down_one),
        ALONG: jnp.where(side == 0, up_two, down_two),
        RELAYED: jnp.where(side == 0, down_two, up_two),
        PASSED: jnp.where(core == 0, down_one, up_one),
    }
    spread = {slot: jnp.concatenate([row] * (size // 128), axis=1) for slot, row in chosen.items()}
    eight = sums[OWN]
    for slot in (PEER, ALONG, RELAYED, PASSED):
        eight = eight + spread[slot] * sums[slot]
    degrees = jnp.sum(eight, axis=0, keepdims=True)
    degree_ref[...] = degrees
    scale = lax.rsqrt(degrees)
    load_start.wait()

    def block_copy(step, buffer, target, cut):
        length = size // cuts
        at = (slice(None), pl.ds(cut * length, length))
        source, device = {
            PEER: (OWN, peer),
            ALONG: (OWN, along),
            RELAYED: (ALONG, ahead),
            PASSED: (ALONG + role, peer),
        }[target]
        sems = p_out.at[step, target, cut], p_in.at[step, target, cut]
        return send(buffer, at, source, target, *sems, device)

    def begin(step, buffer):
        for cut in range(cuts):
            block_copy(step, buffer, ALONG, cut).start()
            block_copy(step, buffer, PEER, cut).start()

    def relay(step, buffer, some):
        for cut in some:
            block_copy(step, buffer, ALONG, cut).wait_recv()

            @pl.when(has_ahead)
            def _():
                block_copy(step, buffer, RELAYED, cut).start()

            @pl.when(role == 0)
            def _():
                block_copy(step, buffer, PASSED, cut).start()

    def relay_again(step, buffer, some):
        @pl.when(has_behind)
        def _():
            for cut in some:
                block_copy(step, buffer, RELAYED, cut).wait_recv()

                @pl.when(role == 1)
                def _():
                    block_copy(step, buffer, PASSED, cut).start()

    def product(buffer, slot):
        block = buffer[slot]
        if slot != OWN:
            block = block * spread[slot].astype(jnp.bfloat16)
        return lax.dot_general(block, tile[slot], ROWS_CONTRACTED, preferred_element_type=jnp.float32)

    def early(step, buffer):
        for cut in range(cuts):
            block_copy(step, buffer, PEER, cut).wait_recv()
        acc[: buffer.shape[1]] = product(buffer, OWN) + product(buffer, PEER)

    def late(step, buffer):
        count = buffer.shape[1]

        @pl.when(has_behind)
        def _():
            acc[:count] += product(buffer, RELAYED)

        @pl.when(has_passed)
        def _():
            for cut in range(cuts):
                block_copy(step, buffer, PASSED, cut).wait_recv()
            acc[:count] += product(buffer, PASSED)

    def gram_of(values):
        return lax.dot_general(
            values, values, LAST_CONTRACTED, precision=HIGH, preferred_element_type=jnp.float32
        )

    def phase_of(step, phase):
        return Phase(found[phase], box.at[step, phase], send_sem.at[step, phase], recv_sem.at[step, phase])

    def applied(inverse, values):
        return lax.dot_general(
            inverse, values, ROWS_CONTRACTED, precision=HIGH, preferred_element_type=jnp.float32
        )

    every = range(cuts)
    first[OWN] = (start_ref[...] * scale).astype(jnp.bfloat16)
    begin(0, first)
    early(0, first)
    relay(0, first, every)
    acc[: first.shape[1]] += product(first, ALONG)
    relay_again(0, first, every)
    late(0, first)

    count = first.shape[1]
    normed[...] = acc[:count] * scale
    value = pack(gram_of(normed[...]))
    phases = [phase_of(0, phase) for phase in range(len(found))]
    phases[0].send(value)
    again = normed[...] * scale
    coarse = again.astype(jnp.bfloat16)
    second[OWN, :count] = coarse
    second[OWN, count:] = (again - coarse.astype(jnp.float32)).astype(jnp.bfloat16)
    begin(1, second)
    value = phases[0].receive()
    for phase in phases[1:]:
        phase.send(value)
        if phase is not phases[-1]:
            value = phase.receive()
    half = cuts // 2
    relay(1, second, every[:half])
    early(1, second)
    relay(1, second, every[half:])
    value = phases[-1].receive()
    acc[...] += product(second, ALONG)
    size_of = count // 4
    inverse = inverse_factor(
        unpack(value),
        {
            size_of: lambda: relay_again(1, second, every[:half]),
            2 * size_of: lambda: relay_again(1, second, every[half:]),
        },
    )
    late(1, second)
    image = (acc[:count] + acc[count:]) * scale
    normed[...] = applied(inverse, image)
    value = pack(gram_of(normed[...]))
    for phase in range(len(found)):
        now = phase_of(1, phase)
        now.send(value)
        value = now.receive()
        phases.append(now)
    out_ref[...] = applied(inverse_factor(unpack(value), {}), normed[...])
    for phase in phases:
        phase.settle()

    def settle(step, carry):
        unit_copy(ALONG, step).wait_send()
        unit_copy(PEER, step).wait_send()

        @pl.when(has_ahead)
        def _():
            unit_copy(RELAYED, step).wait_send()

        @pl.when((role == 0) | has_behind)
        def _():
            unit_copy(PASSED, step).wait_send()

        return carry

    lax.fori_loop(0, parts, settle, 0)
    for offset in range(1, W + 1):

        @pl.when(me + offset < peers)
        def _():
            keep_copy(offset).wait_send()

    for step, buffer in enumerate((first, second)):
        for cut in range(cuts):
            block_copy(step, buffer, ALONG, cut).wait_send()
            block_copy(step, buffer, PEER, cut).wait_send()

            @pl.when(has_ahead)
            def _():
                block_copy(step, buffer, RELAYED, cut).wait_send()

            @pl.when((role == 0) | has_behind)
            def _():
                block_copy(step, buffer, PASSED, cut).wait_send()


def local(peers, features, iterate, band_mask):
    size, depth = features.shape
    count = iterate.shape[1]
    plan = radices(peers)
    phases, widest = len(plan), max(plan)
    parts, cuts = PARTS, CUTS
    dma = pltpu.SemaphoreType.DMA
    current, degrees = pl.pallas_call(
        functools.partial(fused_kernel, plan, peers, parts, cuts),
        out_shape=(
            jax.ShapeDtypeStruct((count, size), jnp.float32),
            jax.ShapeDtypeStruct((1, size), jnp.float32),
        ),
        in_specs=[pl.BlockSpec(memory_space=pl.ANY)] * 3,
        out_specs=(pl.BlockSpec(memory_space=pltpu.VMEM),) * 2,
        scratch_shapes=[
            pltpu.VMEM((size, depth), jnp.bfloat16),
            pltpu.VMEM((count, size), jnp.float32),
            pltpu.VMEM(band_mask.shape, jnp.int32),
            pltpu.VMEM((5, size, depth), jnp.bfloat16),
            pltpu.VMEM((depth, size), jnp.bfloat16),
            pltpu.VMEM((5, size, size), jnp.bfloat16),
            pltpu.VMEM((5, 8, size), jnp.float32),
            pltpu.VMEM((1 + W, 8, 128), jnp.float32),
            pltpu.VMEM((2 * count, size), jnp.float32),
            pltpu.VMEM((count, size), jnp.float32),
            pltpu.VMEM((5, count, size), jnp.bfloat16),
            pltpu.VMEM((5, 2 * count, size), jnp.bfloat16),
            pltpu.VMEM((ITERS, phases, widest, count // 2, 2 * count), jnp.float32),
            dma((3,)),
            dma((5, parts)),
            dma((5, parts)),
            dma((1 + W,)),
            dma((1 + W,)),
            dma((ITERS, 5, cuts)),
            dma((ITERS, 5, cuts)),
            dma((ITERS, phases, widest)),
            dma((ITERS, phases, widest)),
        ],
        compiler_params=pltpu.CompilerParams(
            collective_id=0, has_side_effects=True, vmem_limit_bytes=48 << 20
        ),
        name="fused",
    )(features, iterate.T, band_mask)
    return (current.T, degrees[0])


def solution(mesh):
    return jax.shard_map(
        functools.partial(local, mesh.shape[AXIS]),
        mesh=mesh,
        in_specs=(
            P(("groups", "rows"), None),
            P(("groups", "rows"), None),
            P(("groups", "rows"), None),
        ),
        out_specs=(P(("groups", "rows"), None), P(("groups", "rows"))),
        check_vma=False,
    )
```

```python
import functools

import jax
import jax.numpy as jnp
from jax import lax
from jax.experimental import pallas as pl
from jax.experimental.pallas import tpu as pltpu
from jax.sharding import PartitionSpec as P

W = 2
ITERS = 2
PARTS = 8
CUTS = 4
AXIS = "rows"
MESH = pl.DeviceIdType.MESH
HIGH = lax.Precision.HIGHEST


def radices(count):
    out = []
    while count > 1:
        radix = next((r for r in (4, 2, 3, 5, 7) if count % r == 0), count)
        out.append(radix)
        count //= radix
    return out


def peers_of(me, plan):
    stride = 1
    found = []
    for radix in plan:
        digit = lax.rem(lax.div(me, stride), radix)
        row = []
        for k in range(1, radix):
            other = lax.rem(digit + k, radix)
            row.append((other, me + (other - digit) * stride))
        found.append((digit, row))
        stride *= radix
    return found


class Phase:
    def __init__(self, found, box, send_sem, recv_sem):
        self.digit, self.row = found
        self.box, self.send_sem, self.recv_sem = box, send_sem, recv_sem

    def copy(self, k, slot, peer):
        return pltpu.make_async_remote_copy(
            src_ref=self.box.at[slot],
            dst_ref=self.box.at[slot],
            send_sem=self.send_sem.at[k],
            recv_sem=self.recv_sem.at[slot],
            device_id={AXIS: peer},
            device_id_type=MESH,
        )

    def send(self, value):
        self.box[self.digit] = value
        for k, (_, peer) in enumerate(self.row):
            self.copy(k, self.digit, peer).start()

    def receive(self):
        for k, (other, peer) in enumerate(self.row):
            self.copy(k, other, peer).wait_recv()
        value = self.box[0]
        for slot in range(1, len(self.row) + 1):
            value = value + self.box[slot]
        return value

    def settle(self):
        for k, (_, peer) in enumerate(self.row):
            self.copy(k, self.digit, peer).wait_send()


def inverse_factor(gram, pauses):
    size = gram.shape[0]
    rows = lax.broadcasted_iota(jnp.int32, (size, size), 0)
    cols = lax.broadcasted_iota(jnp.int32, (size, size), 1)
    both = jnp.concatenate([gram, jnp.where(rows == cols, 1.0, 0.0)], axis=1)
    count = size // 8
    bands = [both[8 * b : 8 * b + 8] for b in range(count)]
    sub = lax.broadcasted_iota(jnp.int32, (8, 2 * size), 0)
    out = []
    for b in range(count):
        if b in pauses:
            pauses[b]()
        panel = {
            c: [jnp.broadcast_to(bands[c][:, 8 * b + k : 8 * b + k + 1], (8, 2 * size)) for k in range(8)]
            for c in range(b, count)
        }
        diagonal = jnp.ones((8, 2 * size), jnp.float32)
        for k in range(8):
            pivot = panel[b][k][k : k + 1]
            inverse = 1.0 / pivot
            diagonal = jnp.where(sub == k, pivot, diagonal)
            row = bands[b][k : k + 1] * inverse
            heads = [panel[b][j][k : k + 1] * inverse for j in range(k + 1, 8)]
            for c in range(b, count):
                column = panel[c][k]
                if c == b:
                    column = jnp.where(sub > k, column, 0.0)
                bands[c] = bands[c] - column * row
                for j in range(k + 1, 8):
                    panel[c][j] = panel[c][j] - column * heads[j - k - 1]
        out.append((bands[b] * lax.rsqrt(diagonal))[:, size:])
    return jnp.concatenate(out, axis=0)


def pack(gram):
    half = gram.shape[0] // 2
    return jnp.concatenate([gram[:half], gram[half:]], axis=1)


def unpack(packed):
    size = packed.shape[1] // 2
    return jnp.concatenate([packed[:, :size], packed[:, size:]], axis=0)


OWN, PEER, ALONG, RELAYED, PASSED = range(5)
ROWS_CONTRACTED = (((1,), (0,)), ((), ()))
LAST_CONTRACTED = (((1,), (1,)), ((), ()))


def fused_kernel(plan, peers, parts, cuts, feature_hbm, start_hbm, mask_hbm, *refs):
    out_ref, degree_ref = refs[:2]
    feature_ref, start_ref, mask_ref, unit, flipped, tile, sums, keep, acc, normed, first, second, box = refs[2:15]
    loads, u_out, u_in, k_out, k_in, p_out, p_in, send_sem, recv_sem = refs[15:]
    load_feature = pltpu.make_async_copy(feature_hbm, feature_ref, loads.at[0])
    load_mask = pltpu.make_async_copy(mask_hbm, mask_ref, loads.at[1])
    load_start = pltpu.make_async_copy(start_hbm, start_ref, loads.at[2])
    load_feature.start()
    load_mask.start()
    load_start.start()
    me = lax.axis_index(AXIS)
    core = lax.rem(me, 2)
    side = lax.rem(lax.div(me, 2), 2)
    role = core + side - 2 * core * side
    peer = me + 1 - 2 * core
    along = me + 2 - 4 * side
    ahead = me + 4 - 8 * side
    behind = me - 4 + 8 * side
    has_ahead = (ahead >= 0) & (ahead < peers)
    has_behind = (behind >= 0) & (behind < peers)
    has_passed = (role == 1) | has_behind
    found = peers_of(me, plan)

    keep[1] = jnp.zeros((8, 128), jnp.float32)
    keep[2] = jnp.zeros((8, 128), jnp.float32)

    barrier = pltpu.get_barrier_semaphore()
    total = 0
    for _, row in found:
        for _, other in row:
            pl.semaphore_signal(barrier, inc=1, device_id={AXIS: other}, device_id_type=MESH)
            total += 1
    for offset in (1, 2, 4):

        @pl.when(me >= offset)
        def _():
            pl.semaphore_signal(barrier, inc=1, device_id={AXIS: me - offset}, device_id_type=MESH)

        @pl.when(me + offset < peers)
        def _():
            pl.semaphore_signal(barrier, inc=1, device_id={AXIS: me + offset}, device_id_type=MESH)

        total = total + (me >= offset).astype(jnp.int32) + (me + offset < peers).astype(jnp.int32)

    size = feature_ref.shape[0]
    width = size // parts
    sums[...] = jnp.zeros_like(sums)
    load_feature.wait()

    def normalise(step, carry):
        at = pl.ds(pl.multiple_of(step * width, width), width)
        values = feature_ref[at].astype(jnp.float32)
        square = jnp.sum(values * values, axis=-1, keepdims=True)
        unit[OWN, at] = (values * lax.rsqrt(square + 1e-06)).astype(jnp.bfloat16)
        return carry

    lax.fori_loop(0, parts, normalise, 0)
    pl.semaphore_wait(barrier, total)

    def send(buffer, at, source, target, out_sem, in_sem, device):
        return pltpu.make_async_remote_copy(
            src_ref=buffer.at[(source,) + at],
            dst_ref=buffer.at[(target,) + at],
            send_sem=out_sem,
            recv_sem=in_sem,
            device_id={AXIS: device},
            device_id_type=MESH,
        )

    def unit_copy(target, step):
        at = (pl.ds(pl.multiple_of(step * width, width), width),)
        source, device = {
            PEER: (OWN, peer),
            ALONG: (OWN, along),
            RELAYED: (ALONG, ahead),
            PASSED: (ALONG + role, peer),
        }[target]
        sems = u_out.at[target, step], u_in.at[target, step]
        return send(unit, at, source, target, *sems, device)

    def keep_copy(offset):
        return send(keep, (), 0, offset, k_out.at[offset], k_in.at[offset], me + offset)

    def launch(step, carry):
        unit_copy(ALONG, step).start()
        unit_copy(PEER, step).start()
        return carry

    lax.fori_loop(0, parts, launch, 0)
    load_mask.wait()
    row_at = lax.broadcasted_iota(jnp.int32, (8, 128), 0)
    flags = mask_ref[...].astype(jnp.float32)
    keep[0] = jnp.where(row_at == 0, flags[:, 0:1], jnp.where(row_at == 1, flags[:, 1:2], 0.0))
    flipped[...] = unit[OWN].T
    for offset in range(1, W + 1):

        @pl.when(me + offset < peers)
        def _():
            keep_copy(offset).start()

    def piece(slot, step):
        at = pl.ds(pl.multiple_of(step * width, width), width)
        scores = lax.dot_general(
            unit[slot, at], flipped[...], ROWS_CONTRACTED, preferred_element_type=jnp.float32
        )
        values = jnp.exp(scores).astype(jnp.bfloat16)
        tile[slot, at] = values
        sums[slot] += jnp.sum(values.astype(jnp.float32).reshape(width // 8, 8, size), axis=0)

    def turn(step, carry):
        @pl.when(step < parts)
        def _():
            unit_copy(ALONG, step).wait_recv()

            @pl.when(has_ahead)
            def _():
                unit_copy(RELAYED, step).start()

            @pl.when(role == 0)
            def _():
                unit_copy(PASSED, step).start()

            unit_copy(PEER, step).wait_recv()
            piece(ALONG, step)
            piece(OWN, step)
            piece(PEER, step)

        @pl.when((step >= 1) & (step <= parts) & has_behind)
        def _():
            unit_copy(RELAYED, step - 1).wait_recv()

            @pl.when(role == 1)
            def _():
                unit_copy(PASSED, step - 1).start()

            piece(RELAYED, step - 1)

        @pl.when((step >= 2) & has_passed)
        def _():
            unit_copy(PASSED, step - 2).wait_recv()
            piece(PASSED, step - 2)

        return carry

    lax.fori_loop(0, parts + 2, turn, 0)

    for offset in range(1, W + 1):

        @pl.when(me >= offset)
        def _():
            keep_copy(offset).wait_recv()

    up_one, up_two = keep[0][0:1], keep[0][1:2]
    down_one, down_two = keep[1][0:1], keep[2][1:2]
    chosen = {
        PEER: jnp.where(core == 0, up_one, down_one),
        ALONG: jnp.where(side == 0, up_two, down_two),
        RELAYED: jnp.where(side == 0, down_two, up_two),
        PASSED: jnp.where(core == 0, down_one, up_one),
    }
    spread = {slot: jnp.concatenate([row] * (size // 128), axis=1) for slot, row in chosen.items()}
    eight = sums[OWN]
    for slot in (PEER, ALONG, RELAYED, PASSED):
        eight = eight + spread[slot] * sums[slot]
    degrees = jnp.sum(eight, axis=0, keepdims=True)
    degree_ref[...] = degrees
    scale = lax.rsqrt(degrees)
    load_start.wait()

    def block_copy(step, buffer, target, cut):
        length = size // cuts
        at = (slice(None), pl.ds(cut * length, length))
        source, device = {
            PEER: (OWN, peer),
            ALONG: (OWN, along),
            RELAYED: (ALONG, ahead),
            PASSED: (ALONG + role, peer),
        }[target]
        sems = p_out.at[step, target, cut], p_in.at[step, target, cut]
        return send(buffer, at, source, target, *sems, device)

    def begin(step, buffer):
        for cut in range(cuts):
            block_copy(step, buffer, ALONG, cut).start()
            block_copy(step, buffer, PEER, cut).start()

    def relay(step, buffer, some):
        for cut in some:
            block_copy(step, buffer, ALONG, cut).wait_recv()

            @pl.when(has_ahead)
            def _():
                block_copy(step, buffer, RELAYED, cut).start()

            @pl.when(role == 0)
            def _():
                block_copy(step, buffer, PASSED, cut).start()

    def relay_again(step, buffer, some):
        @pl.when(has_behind)
        def _():
            for cut in some:
                block_copy(step, buffer, RELAYED, cut).wait_recv()

                @pl.when(role == 1)
                def _():
                    block_copy(step, buffer, PASSED, cut).start()

    def product(buffer, slot):
        block = buffer[slot]
        if slot != OWN:
            block = block * spread[slot].astype(jnp.bfloat16)
        return lax.dot_general(block, tile[slot], ROWS_CONTRACTED, preferred_element_type=jnp.float32)

    def early(step, buffer):
        for cut in range(cuts):
            block_copy(step, buffer, PEER, cut).wait_recv()
        acc[: buffer.shape[1]] = product(buffer, OWN) + product(buffer, PEER)

    def late(step, buffer):
        count = buffer.shape[1]

        @pl.when(has_behind)
        def _():
            acc[:count] += product(buffer, RELAYED)

        @pl.when(has_passed)
        def _():
            for cut in range(cuts):
                block_copy(step, buffer, PASSED, cut).wait_recv()
            acc[:count] += product(buffer, PASSED)

    def gram_of(values):
        return lax.dot_general(
            values, values, LAST_CONTRACTED, precision=HIGH, preferred_element_type=jnp.float32
        )

    def phase_of(step, phase):
        return Phase(found[phase], box.at[step, phase], send_sem.at[step, phase], recv_sem.at[step, phase])

    def applied(inverse, values):
        return lax.dot_general(
            inverse, values, ROWS_CONTRACTED, precision=HIGH, preferred_element_type=jnp.float32
        )

    every = range(cuts)
    first[OWN] = (start_ref[...] * scale).astype(jnp.bfloat16)
    begin(0, first)
    early(0, first)
    relay(0, first, every)
    acc[: first.shape[1]] += product(first, ALONG)
    relay_again(0, first, every)
    late(0, first)

    count = first.shape[1]
    normed[...] = acc[:count] * scale
    value = pack(gram_of(normed[...]))
    phases = [phase_of(0, phase) for phase in range(len(found))]
    phases[0].send(value)
    again = normed[...] * scale
    coarse = again.astype(jnp.bfloat16)
    second[OWN, :count] = coarse
    second[OWN, count:] = (again - coarse.astype(jnp.float32)).astype(jnp.bfloat16)
    begin(1, second)
    value = phases[0].receive()
    for phase in phases[1:]:
        phase.send(value)
        if phase is not phases[-1]:
            value = phase.receive()
    half = cuts // 2
    relay(1, second, every[:half])
    early(1, second)
    relay(1, second, every[half:])
    value = phases[-1].receive()
    acc[...] += product(second, ALONG)
    quarter = count // 32
    inverse = inverse_factor(
        unpack(value),
        {
            quarter: lambda: relay_again(1, second, every[:half]),
            2 * quarter: lambda: relay_again(1, second, every[half:]),
        },
    )
    late(1, second)
    image = (acc[:count] + acc[count:]) * scale
    normed[...] = applied(inverse, image)
    value = pack(gram_of(normed[...]))
    for phase in range(len(found)):
        now = phase_of(1, phase)
        now.send(value)
        value = now.receive()
        phases.append(now)
    out_ref[...] = applied(inverse_factor(unpack(value), {}), normed[...])
    for phase in phases:
        phase.settle()

    def settle(step, carry):
        unit_copy(ALONG, step).wait_send()
        unit_copy(PEER, step).wait_send()

        @pl.when(has_ahead)
        def _():
            unit_copy(RELAYED, step).wait_send()

        @pl.when((role == 0) | has_behind)
        def _():
            unit_copy(PASSED, step).wait_send()

        return carry

    lax.fori_loop(0, parts, settle, 0)
    for offset in range(1, W + 1):

        @pl.when(me + offset < peers)
        def _():
            keep_copy(offset).wait_send()

    for step, buffer in enumerate((first, second)):
        for cut in range(cuts):
            block_copy(step, buffer, ALONG, cut).wait_send()
            block_copy(step, buffer, PEER, cut).wait_send()

            @pl.when(has_ahead)
            def _():
                block_copy(step, buffer, RELAYED, cut).wait_send()

            @pl.when((role == 0) | has_behind)
            def _():
                block_copy(step, buffer, PASSED, cut).wait_send()


def local(peers, features, iterate, band_mask):
    size, depth = features.shape
    count = iterate.shape[1]
    plan = radices(peers)
    phases, widest = len(plan), max(plan)
    parts, cuts = PARTS, CUTS
    dma = pltpu.SemaphoreType.DMA
    current, degrees = pl.pallas_call(
        functools.partial(fused_kernel, plan, peers, parts, cuts),
        out_shape=(
            jax.ShapeDtypeStruct((count, size), jnp.float32),
            jax.ShapeDtypeStruct((1, size), jnp.float32),
        ),
        in_specs=[pl.BlockSpec(memory_space=pltpu.HBM)] * 3,
        out_specs=(pl.BlockSpec(memory_space=pltpu.VMEM),) * 2,
        scratch_shapes=[
            pltpu.VMEM((size, depth), jnp.bfloat16),
            pltpu.VMEM((count, size), jnp.float32),
            pltpu.VMEM(band_mask.shape, jnp.int32),
            pltpu.VMEM((5, size, depth), jnp.bfloat16),
            pltpu.VMEM((depth, size), jnp.bfloat16),
            pltpu.VMEM((5, size, size), jnp.bfloat16),
            pltpu.VMEM((5, 8, size), jnp.float32),
            pltpu.VMEM((1 + W, 8, 128), jnp.float32),
            pltpu.VMEM((2 * count, size), jnp.float32),
            pltpu.VMEM((count, size), jnp.float32),
            pltpu.VMEM((5, count, size), jnp.bfloat16),
            pltpu.VMEM((5, 2 * count, size), jnp.bfloat16),
            pltpu.VMEM((ITERS, phases, widest, count // 2, 2 * count), jnp.float32),
            dma((3,)),
            dma((5, parts)),
            dma((5, parts)),
            dma((1 + W,)),
            dma((1 + W,)),
            dma((ITERS, 5, cuts)),
            dma((ITERS, 5, cuts)),
            dma((ITERS, phases, widest)),
            dma((ITERS, phases, widest)),
        ],
        compiler_params=pltpu.CompilerParams(
            collective_id=0, has_side_effects=True, vmem_limit_bytes=48 << 20
        ),
        name="fused",
    )(features, iterate.T, band_mask)
    return (current.T, degrees[0])


def solution(mesh):
    return jax.shard_map(
        functools.partial(local, mesh.shape[AXIS]),
        mesh=mesh,
        in_specs=(
            P(("groups", "rows"), None),
            P(("groups", "rows"), None),
            P(("groups", "rows"), None),
        ),
        out_specs=(P(("groups", "rows"), None), P(("groups", "rows"))),
        check_vma=False,
    )
```

```python
import functools

import jax
import jax.numpy as jnp
from jax import lax
from jax.experimental import pallas as pl
from jax.experimental.pallas import tpu as pltpu
from jax.sharding import PartitionSpec as P

W = 2
ITERS = 2
PARTS = 8
CUTS = 4
AXIS = "rows"
MESH = pl.DeviceIdType.MESH
HIGH = lax.Precision.HIGHEST


def radices(count):
    out = []
    while count > 1:
        radix = next((r for r in (4, 2, 3, 5, 7) if count % r == 0), count)
        out.append(radix)
        count //= radix
    return out


def peers_of(me, plan):
    stride = 1
    found = []
    for radix in plan:
        digit = lax.rem(lax.div(me, stride), radix)
        row = []
        for k in range(1, radix):
            other = lax.rem(digit + k, radix)
            row.append((other, me + (other - digit) * stride))
        found.append((digit, row))
        stride *= radix
    return found


class Phase:
    def __init__(self, found, box, send_sem, recv_sem):
        self.digit, self.row = found
        self.box, self.send_sem, self.recv_sem = box, send_sem, recv_sem

    def copy(self, k, slot, peer):
        return pltpu.make_async_remote_copy(
            src_ref=self.box.at[slot],
            dst_ref=self.box.at[slot],
            send_sem=self.send_sem.at[k],
            recv_sem=self.recv_sem.at[slot],
            device_id={AXIS: peer},
            device_id_type=MESH,
        )

    def send(self, value):
        self.box[self.digit] = value
        for k, (_, peer) in enumerate(self.row):
            self.copy(k, self.digit, peer).start()

    def receive(self):
        for k, (other, peer) in enumerate(self.row):
            self.copy(k, other, peer).wait_recv()
        value = self.box[0]
        for slot in range(1, len(self.row) + 1):
            value = value + self.box[slot]
        return value

    def settle(self):
        for k, (_, peer) in enumerate(self.row):
            self.copy(k, self.digit, peer).wait_send()


def inverse_factor(gram, pauses):
    size = gram.shape[0]
    rows = lax.broadcasted_iota(jnp.int32, (size, size), 0)
    cols = lax.broadcasted_iota(jnp.int32, (size, size), 1)
    both = jnp.concatenate([gram, jnp.where(rows == cols, 1.0, 0.0)], axis=1)
    count = size // 8
    bands = [both[8 * b : 8 * b + 8] for b in range(count)]
    sub = lax.broadcasted_iota(jnp.int32, (8, 2 * size), 0)
    out = []
    for b in range(count):
        if b in pauses:
            pauses[b]()
        panel = {
            c: [jnp.broadcast_to(bands[c][:, 8 * b + k : 8 * b + k + 1], (8, 2 * size)) for k in range(8)]
            for c in range(b, count)
        }
        diagonal = jnp.ones((8, 2 * size), jnp.float32)
        for k in range(8):
            pivot = panel[b][k][k : k + 1]
            inverse = 1.0 / pivot
            diagonal = jnp.where(sub == k, pivot, diagonal)
            row = bands[b][k : k + 1] * inverse
            heads = [panel[b][j][k : k + 1] * inverse for j in range(k + 1, 8)]
            for c in range(b, count):
                column = panel[c][k]
                if c == b:
                    column = jnp.where(sub > k, column, 0.0)
                bands[c] = bands[c] - column * row
                for j in range(k + 1, 8):
                    panel[c][j] = panel[c][j] - column * heads[j - k - 1]
        out.append((bands[b] * lax.rsqrt(diagonal))[:, size:])
    return jnp.concatenate(out, axis=0)


def pack(gram):
    half = gram.shape[0] // 2
    return jnp.concatenate([gram[:half], gram[half:]], axis=1)


def unpack(packed):
    size = packed.shape[1] // 2
    return jnp.concatenate([packed[:, :size], packed[:, size:]], axis=0)


OWN, PEER, ALONG, RELAYED, PASSED = range(5)
ROWS_CONTRACTED = (((1,), (0,)), ((), ()))
LAST_CONTRACTED = (((1,), (1,)), ((), ()))


def fused_kernel(plan, peers, parts, cuts, feature_hbm, start_hbm, mask_hbm, *refs):
    out_ref, degree_ref = refs[:2]
    feature_ref, start_ref, mask_ref, unit, flipped, tile, sums, keep, acc, normed, first, second, box = refs[2:15]
    loads, u_out, u_in, k_out, k_in, p_out, p_in, send_sem, recv_sem = refs[15:]
    load_feature = pltpu.make_async_copy(feature_hbm, feature_ref, loads.at[0])
    load_mask = pltpu.make_async_copy(mask_hbm, mask_ref, loads.at[1])
    load_start = pltpu.make_async_copy(start_hbm, start_ref, loads.at[2])
    load_feature.start()
    load_mask.start()
    load_start.start()
    me = lax.axis_index(AXIS)
    core = lax.rem(me, 2)
    side = lax.rem(lax.div(me, 2), 2)
    role = core + side - 2 * core * side
    peer = me + 1 - 2 * core
    along = me + 2 - 4 * side
    ahead = me + 4 - 8 * side
    behind = me - 4 + 8 * side
    has_ahead = (ahead >= 0) & (ahead < peers)
    has_behind = (behind >= 0) & (behind < peers)
    has_passed = (role == 1) | has_behind
    found = peers_of(me, plan)

    keep[1] = jnp.zeros((8, 128), jnp.float32)
    keep[2] = jnp.zeros((8, 128), jnp.float32)

    barrier = pltpu.get_barrier_semaphore()
    total = 0
    for _, row in found:
        for _, other in row:
            pl.semaphore_signal(barrier, inc=1, device_id={AXIS: other}, device_id_type=MESH)
            total += 1
    for offset in (1, 2, 4):

        @pl.when(me >= offset)
        def _():
            pl.semaphore_signal(barrier, inc=1, device_id={AXIS: me - offset}, device_id_type=MESH)

        @pl.when(me + offset < peers)
        def _():
            pl.semaphore_signal(barrier, inc=1, device_id={AXIS: me + offset}, device_id_type=MESH)

        total = total + (me >= offset).astype(jnp.int32) + (me + offset < peers).astype(jnp.int32)

    size = feature_ref.shape[0]
    width = size // parts
    sums[...] = jnp.zeros_like(sums)
    load_feature.wait()

    def normalise(step, carry):
        at = pl.ds(pl.multiple_of(step * width, width), width)
        values = feature_ref[at].astype(jnp.float32)
        square = jnp.sum(values * values, axis=-1, keepdims=True)
        unit[OWN, at] = (values * lax.rsqrt(square + 1e-06)).astype(jnp.bfloat16)
        return carry

    lax.fori_loop(0, parts, normalise, 0)
    pl.semaphore_wait(barrier, total)

    def send(buffer, at, source, target, out_sem, in_sem, device):
        return pltpu.make_async_remote_copy(
            src_ref=buffer.at[(source,) + at],
            dst_ref=buffer.at[(target,) + at],
            send_sem=out_sem,
            recv_sem=in_sem,
            device_id={AXIS: device},
            device_id_type=MESH,
        )

    def unit_copy(target, step):
        at = (pl.ds(pl.multiple_of(step * width, width), width),)
        source, device = {
            PEER: (OWN, peer),
            ALONG: (OWN, along),
            RELAYED: (ALONG, ahead),
            PASSED: (ALONG + role, peer),
        }[target]
        sems = u_out.at[target, step], u_in.at[target, step]
        return send(unit, at, source, target, *sems, device)

    def keep_copy(offset):
        return send(keep, (), 0, offset, k_out.at[offset], k_in.at[offset], me + offset)

    def launch(step, carry):
        unit_copy(ALONG, step).start()
        unit_copy(PEER, step).start()
        return carry

    lax.fori_loop(0, parts, launch, 0)
    load_mask.wait()
    row_at = lax.broadcasted_iota(jnp.int32, (8, 128), 0)
    flags = mask_ref[...].astype(jnp.float32)
    keep[0] = jnp.where(row_at == 0, flags[:, 0:1], jnp.where(row_at == 1, flags[:, 1:2], 0.0))
    flipped[...] = unit[OWN].T
    for offset in range(1, W + 1):

        @pl.when(me + offset < peers)
        def _():
            keep_copy(offset).start()

    def piece(slot, step):
        at = pl.ds(pl.multiple_of(step * width, width), width)
        scores = lax.dot_general(
            unit[slot, at], flipped[...], ROWS_CONTRACTED, preferred_element_type=jnp.float32
        )
        values = jnp.exp(scores).astype(jnp.bfloat16)
        tile[slot, at] = values
        sums[slot] += jnp.sum(values.astype(jnp.float32).reshape(width // 8, 8, size), axis=0)

    def turn(step, carry):
        @pl.when(step < parts)
        def _():
            unit_copy(ALONG, step).wait_recv()

            @pl.when(has_ahead)
            def _():
                unit_copy(RELAYED, step).start()

            @pl.when(role == 0)
            def _():
                unit_copy(PASSED, step).start()

            unit_copy(PEER, step).wait_recv()
            piece(ALONG, step)
            piece(OWN, step)
            piece(PEER, step)

        @pl.when((step >= 1) & (step <= parts) & has_behind)
        def _():
            unit_copy(RELAYED, step - 1).wait_recv()

            @pl.when(role == 1)
            def _():
                unit_copy(PASSED, step - 1).start()

            piece(RELAYED, step - 1)

        @pl.when((step >= 2) & has_passed)
        def _():
            unit_copy(PASSED, step - 2).wait_recv()
            piece(PASSED, step - 2)

        return carry

    lax.fori_loop(0, parts + 2, turn, 0)

    for offset in range(1, W + 1):

        @pl.when(me >= offset)
        def _():
            keep_copy(offset).wait_recv()

    up_one, up_two = keep[0][0:1], keep[0][1:2]
    down_one, down_two = keep[1][0:1], keep[2][1:2]
    chosen = {
        PEER: jnp.where(core == 0, up_one, down_one),
        ALONG: jnp.where(side == 0, up_two, down_two),
        RELAYED: jnp.where(side == 0, down_two, up_two),
        PASSED: jnp.where(core == 0, down_one, up_one),
    }
    spread = {slot: jnp.concatenate([row] * (size // 128), axis=1) for slot, row in chosen.items()}
    columns = {slot: jnp.sum(sums[slot], axis=0, keepdims=True) for slot in range(5)}
    for slot, flag in spread.items():
        columns[slot] = flag * columns[slot]
    degrees = columns[OWN] + columns[PEER] + columns[ALONG] + columns[RELAYED] + columns[PASSED]
    degree_ref[...] = degrees
    scale = lax.rsqrt(degrees)
    load_start.wait()

    def block_copy(step, buffer, target, cut):
        units = buffer.shape[2] // 128
        low, high = -(-units * cut // cuts), -(-units * (cut + 1) // cuts)
        at = (slice(None), pl.ds(low * 128, (high - low) * 128))
        source, device = {
            PEER: (OWN, peer),
            ALONG: (OWN, along),
            RELAYED: (ALONG, ahead),
            PASSED: (ALONG + role, peer),
        }[target]
        sems = p_out.at[step, target, cut], p_in.at[step, target, cut]
        return send(buffer, at, source, target, *sems, device)

    def begin(step, buffer):
        for cut in range(cuts):
            block_copy(step, buffer, ALONG, cut).start()
            block_copy(step, buffer, PEER, cut).start()

    def relay(step, buffer, some):
        for cut in some:
            block_copy(step, buffer, ALONG, cut).wait_recv()

            @pl.when(has_ahead)
            def _():
                block_copy(step, buffer, RELAYED, cut).start()

            @pl.when(role == 0)
            def _():
                block_copy(step, buffer, PASSED, cut).start()

    def relay_again(step, buffer, some):
        @pl.when(has_behind)
        def _():
            for cut in some:
                block_copy(step, buffer, RELAYED, cut).wait_recv()

                @pl.when(role == 1)
                def _():
                    block_copy(step, buffer, PASSED, cut).start()

    def product(buffer, slot):
        block = buffer[slot, :, :size]
        if slot != OWN:
            block = block * spread[slot].astype(jnp.bfloat16)
        value = lax.dot_general(block, tile[slot], ROWS_CONTRACTED, preferred_element_type=jnp.float32)
        if buffer.shape[2] > size:
            value = value + buffer[slot, :, size : size + 1].astype(jnp.float32) * columns[slot]
        return value

    def early(step, buffer):
        for cut in range(cuts):
            block_copy(step, buffer, PEER, cut).wait_recv()
        acc[...] = product(buffer, OWN) + product(buffer, PEER)

    def late(step, buffer):
        @pl.when(has_behind)
        def _():
            acc[...] += product(buffer, RELAYED)

        @pl.when(has_passed)
        def _():
            for cut in range(cuts):
                block_copy(step, buffer, PASSED, cut).wait_recv()
            acc[...] += product(buffer, PASSED)

    def gram_of(values):
        return lax.dot_general(
            values, values, LAST_CONTRACTED, precision=HIGH, preferred_element_type=jnp.float32
        )

    def phase_of(step, phase):
        return Phase(found[phase], box.at[step, phase], send_sem.at[step, phase], recv_sem.at[step, phase])

    def applied(inverse, values):
        return lax.dot_general(
            inverse, values, ROWS_CONTRACTED, precision=HIGH, preferred_element_type=jnp.float32
        )

    every = range(cuts)
    first[OWN] = (start_ref[...] * scale).astype(jnp.bfloat16)
    begin(0, first)
    early(0, first)
    relay(0, first, every)
    acc[...] += product(first, ALONG)
    relay_again(0, first, every)
    late(0, first)

    count = first.shape[1]
    normed[...] = acc[...] * scale
    value = pack(gram_of(normed[...]))
    phases = [phase_of(0, phase) for phase in range(len(found))]
    phases[0].send(value)
    again = normed[...] * scale
    centre = jnp.sum(again, axis=1, keepdims=True) * (1.0 / size)
    centre = jnp.broadcast_to(centre, (count, 128)).astype(jnp.bfloat16)
    second[OWN, :, size:] = centre
    second[OWN, :, :size] = (again - centre[:, 0:1].astype(jnp.float32)).astype(jnp.bfloat16)
    begin(1, second)
    value = phases[0].receive()
    for phase in phases[1:]:
        phase.send(value)
        if phase is not phases[-1]:
            value = phase.receive()
    half = cuts // 2
    relay(1, second, every[:half])
    early(1, second)
    relay(1, second, every[half:])
    value = phases[-1].receive()
    acc[...] += product(second, ALONG)
    quarter = count // 32
    inverse = inverse_factor(
        unpack(value),
        {
            quarter: lambda: relay_again(1, second, every[:half]),
            2 * quarter: lambda: relay_again(1, second, every[half:]),
        },
    )
    late(1, second)
    normed[...] = applied(inverse, acc[...] * scale)
    value = pack(gram_of(normed[...]))
    for phase in range(len(found)):
        now = phase_of(1, phase)
        now.send(value)
        value = now.receive()
        phases.append(now)
    out_ref[...] = applied(inverse_factor(unpack(value), {}), normed[...])
    for phase in phases:
        phase.settle()

    def settle(step, carry):
        unit_copy(ALONG, step).wait_send()
        unit_copy(PEER, step).wait_send()

        @pl.when(has_ahead)
        def _():
            unit_copy(RELAYED, step).wait_send()

        @pl.when((role == 0) | has_behind)
        def _():
            unit_copy(PASSED, step).wait_send()

        return carry

    lax.fori_loop(0, parts, settle, 0)
    for offset in range(1, W + 1):

        @pl.when(me + offset < peers)
        def _():
            keep_copy(offset).wait_send()

    for step, buffer in enumerate((first, second)):
        for cut in range(cuts):
            block_copy(step, buffer, ALONG, cut).wait_send()
            block_copy(step, buffer, PEER, cut).wait_send()

            @pl.when(has_ahead)
            def _():
                block_copy(step, buffer, RELAYED, cut).wait_send()

            @pl.when((role == 0) | has_behind)
            def _():
                block_copy(step, buffer, PASSED, cut).wait_send()


def local(peers, features, iterate, band_mask):
    size, depth = features.shape
    count = iterate.shape[1]
    plan = radices(peers)
    phases, widest = len(plan), max(plan)
    parts, cuts = PARTS, CUTS
    dma = pltpu.SemaphoreType.DMA
    current, degrees = pl.pallas_call(
        functools.partial(fused_kernel, plan, peers, parts, cuts),
        out_shape=(
            jax.ShapeDtypeStruct((count, size), jnp.float32),
            jax.ShapeDtypeStruct((1, size), jnp.float32),
        ),
        in_specs=[pl.BlockSpec(memory_space=pltpu.HBM)] * 3,
        out_specs=(pl.BlockSpec(memory_space=pltpu.VMEM),) * 2,
        scratch_shapes=[
            pltpu.VMEM((size, depth), jnp.bfloat16),
            pltpu.VMEM((count, size), jnp.float32),
            pltpu.VMEM(band_mask.shape, jnp.int32),
            pltpu.VMEM((5, size, depth), jnp.bfloat16),
            pltpu.VMEM((depth, size), jnp.bfloat16),
            pltpu.VMEM((5, size, size), jnp.bfloat16),
            pltpu.VMEM((5, 8, size), jnp.float32),
            pltpu.VMEM((1 + W, 8, 128), jnp.float32),
            pltpu.VMEM((count, size), jnp.float32),
            pltpu.VMEM((count, size), jnp.float32),
            pltpu.VMEM((5, count, size), jnp.bfloat16),
            pltpu.VMEM((5, count, size + 128), jnp.bfloat16),
            pltpu.VMEM((ITERS, phases, widest, count // 2, 2 * count), jnp.float32),
            dma((3,)),
            dma((5, parts)),
            dma((5, parts)),
            dma((1 + W,)),
            dma((1 + W,)),
            dma((ITERS, 5, cuts)),
            dma((ITERS, 5, cuts)),
            dma((ITERS, phases, widest)),
            dma((ITERS, phases, widest)),
        ],
        compiler_params=pltpu.CompilerParams(
            collective_id=0, has_side_effects=True, vmem_limit_bytes=60 << 20
        ),
        name="fused",
    )(features, iterate.T, band_mask)
    return (current.T, degrees[0])


def solution(mesh):
    return jax.shard_map(
        functools.partial(local, mesh.shape[AXIS]),
        mesh=mesh,
        in_specs=(
            P(("groups", "rows"), None),
            P(("groups", "rows"), None),
            P(("groups", "rows"), None),
        ),
        out_specs=(P(("groups", "rows"), None), P(("groups", "rows"))),
        check_vma=False,
    )
```

```python
import functools

import jax
import jax.numpy as jnp
from jax import lax
from jax.experimental import pallas as pl
from jax.experimental.pallas import tpu as pltpu
from jax.sharding import PartitionSpec as P

W = 2
ITERS = 2
PARTS = 8
CUTS = 4
AXIS = "rows"
MESH = pl.DeviceIdType.MESH
HIGH = lax.Precision.HIGHEST


def radices(count):
    out = []
    while count > 1:
        radix = next((r for r in (4, 2, 3, 5, 7) if count % r == 0), count)
        out.append(radix)
        count //= radix
    return out


def peers_of(me, plan):
    stride = 1
    found = []
    for radix in plan:
        digit = lax.rem(lax.div(me, stride), radix)
        row = []
        for k in range(1, radix):
            other = lax.rem(digit + k, radix)
            row.append((other, me + (other - digit) * stride))
        found.append((digit, row))
        stride *= radix
    return found


class Phase:
    def __init__(self, found, box, send_sem, recv_sem):
        self.digit, self.row = found
        self.box, self.send_sem, self.recv_sem = box, send_sem, recv_sem

    def copy(self, k, slot, peer):
        return pltpu.make_async_remote_copy(
            src_ref=self.box.at[slot],
            dst_ref=self.box.at[slot],
            send_sem=self.send_sem.at[k],
            recv_sem=self.recv_sem.at[slot],
            device_id={AXIS: peer},
            device_id_type=MESH,
        )

    def send(self, value):
        self.box[self.digit] = value
        for k, (_, peer) in enumerate(self.row):
            self.copy(k, self.digit, peer).start()

    def receive(self):
        for k, (other, peer) in enumerate(self.row):
            self.copy(k, other, peer).wait_recv()
        value = self.box[0]
        for slot in range(1, len(self.row) + 1):
            value = value + self.box[slot]
        return value

    def settle(self):
        for k, (_, peer) in enumerate(self.row):
            self.copy(k, self.digit, peer).wait_send()


def inverse_factor(gram, pauses):
    size = gram.shape[0]
    rows = lax.broadcasted_iota(jnp.int32, (size, size), 0)
    cols = lax.broadcasted_iota(jnp.int32, (size, size), 1)
    both = jnp.concatenate([gram, jnp.where(rows == cols, 1.0, 0.0)], axis=1)
    count = size // 8
    bands = [both[8 * b : 8 * b + 8] for b in range(count)]
    sub = lax.broadcasted_iota(jnp.int32, (8, 2 * size), 0)
    out = []
    for b in range(count):
        if b in pauses:
            pauses[b]()
        panel = {
            c: [jnp.broadcast_to(bands[c][:, 8 * b + k : 8 * b + k + 1], (8, 2 * size)) for k in range(8)]
            for c in range(b, count)
        }
        diagonal = jnp.ones((8, 2 * size), jnp.float32)
        for k in range(8):
            pivot = panel[b][k][k : k + 1]
            inverse = 1.0 / pivot
            diagonal = jnp.where(sub == k, pivot, diagonal)
            row = bands[b][k : k + 1] * inverse
            heads = [panel[b][j][k : k + 1] * inverse for j in range(k + 1, 8)]
            for c in range(b, count):
                column = panel[c][k]
                if c == b:
                    column = jnp.where(sub > k, column, 0.0)
                bands[c] = bands[c] - column * row
                for j in range(k + 1, 8):
                    panel[c][j] = panel[c][j] - column * heads[j - k - 1]
        out.append((bands[b] * lax.rsqrt(diagonal))[:, size:])
    return jnp.concatenate(out, axis=0)


def pack(gram):
    half = gram.shape[0] // 2
    return jnp.concatenate([gram[:half], gram[half:]], axis=1)


def unpack(packed):
    size = packed.shape[1] // 2
    return jnp.concatenate([packed[:, :size], packed[:, size:]], axis=0)


OWN, PEER, ALONG, RELAYED, PASSED = range(5)
ROWS_CONTRACTED = (((1,), (0,)), ((), ()))
LAST_CONTRACTED = (((1,), (1,)), ((), ()))


def fused_kernel(plan, peers, parts, cuts, feature_hbm, start_hbm, mask_hbm, *refs):
    out_ref, degree_ref = refs[:2]
    feature_ref, starts, mask_ref, unit, flipped, tile, sums, keep, each, acc, normed, second, box = refs[2:15]
    loads, u_out, u_in, k_out, k_in, d_out, d_in, p_out, p_in, send_sem, recv_sem = refs[15:]
    load_feature = pltpu.make_async_copy(feature_hbm, feature_ref, loads.at[0])
    load_mask = pltpu.make_async_copy(mask_hbm, mask_ref, loads.at[1])
    load_start = pltpu.make_async_copy(start_hbm, starts.at[OWN], loads.at[2])
    load_feature.start()
    load_mask.start()
    load_start.start()
    me = lax.axis_index(AXIS)
    core = lax.rem(me, 2)
    side = lax.rem(lax.div(me, 2), 2)
    role = core + side - 2 * core * side
    peer = me + 1 - 2 * core
    along = me + 2 - 4 * side
    ahead = me + 4 - 8 * side
    behind = me - 4 + 8 * side
    has_ahead = (ahead >= 0) & (ahead < peers)
    has_behind = (behind >= 0) & (behind < peers)
    has_passed = (role == 1) | has_behind
    found = peers_of(me, plan)

    keep[1] = jnp.zeros((8, 128), jnp.float32)
    keep[2] = jnp.zeros((8, 128), jnp.float32)

    barrier = pltpu.get_barrier_semaphore()
    total = 0
    for _, row in found:
        for _, other in row:
            pl.semaphore_signal(barrier, inc=1, device_id={AXIS: other}, device_id_type=MESH)
            total += 1
    for offset in (1, 2, 4):

        @pl.when(me >= offset)
        def _():
            pl.semaphore_signal(barrier, inc=1, device_id={AXIS: me - offset}, device_id_type=MESH)

        @pl.when(me + offset < peers)
        def _():
            pl.semaphore_signal(barrier, inc=1, device_id={AXIS: me + offset}, device_id_type=MESH)

        total = total + (me >= offset).astype(jnp.int32) + (me + offset < peers).astype(jnp.int32)

    size = feature_ref.shape[0]
    width = size // parts
    sums[...] = jnp.zeros_like(sums)
    load_feature.wait()

    def normalise(step, carry):
        at = pl.ds(pl.multiple_of(step * width, width), width)
        values = feature_ref[at].astype(jnp.float32)
        square = jnp.sum(values * values, axis=-1, keepdims=True)
        unit[OWN, at] = (values * lax.rsqrt(square + 1e-06)).astype(jnp.bfloat16)
        return carry

    lax.fori_loop(0, parts, normalise, 0)
    pl.semaphore_wait(barrier, total)

    def send(buffer, at, source, target, out_sem, in_sem, device):
        return pltpu.make_async_remote_copy(
            src_ref=buffer.at[(source,) + at],
            dst_ref=buffer.at[(target,) + at],
            send_sem=out_sem,
            recv_sem=in_sem,
            device_id={AXIS: device},
            device_id_type=MESH,
        )

    def unit_copy(target, step):
        at = (pl.ds(pl.multiple_of(step * width, width), width),)
        source, device = {
            PEER: (OWN, peer),
            ALONG: (OWN, along),
            RELAYED: (ALONG, ahead),
            PASSED: (ALONG + role, peer),
        }[target]
        sems = u_out.at[target, step], u_in.at[target, step]
        return send(unit, at, source, target, *sems, device)

    def keep_copy(offset):
        return send(keep, (), 0, offset, k_out.at[offset], k_in.at[offset], me + offset)

    def launch(step, carry):
        unit_copy(ALONG, step).start()
        unit_copy(PEER, step).start()
        return carry

    lax.fori_loop(0, parts, launch, 0)
    load_mask.wait()
    row_at = lax.broadcasted_iota(jnp.int32, (8, 128), 0)
    flags = mask_ref[...].astype(jnp.float32)
    keep[0] = jnp.where(row_at == 0, flags[:, 0:1], jnp.where(row_at == 1, flags[:, 1:2], 0.0))
    flipped[...] = unit[OWN].T
    for offset in range(1, W + 1):

        @pl.when(me + offset < peers)
        def _():
            keep_copy(offset).start()

    def piece(slot, step):
        at = pl.ds(pl.multiple_of(step * width, width), width)
        scores = lax.dot_general(
            unit[slot, at], flipped[...], ROWS_CONTRACTED, preferred_element_type=jnp.float32
        )
        values = jnp.exp(scores).astype(jnp.bfloat16)
        tile[slot, at] = values
        sums[slot] += jnp.sum(values.astype(jnp.float32).reshape(width // 8, 8, size), axis=0)

    def block_copy(step, buffer, target, cut):
        units = buffer.shape[2] // 128
        low, high = -(-units * cut // cuts), -(-units * (cut + 1) // cuts)
        at = (slice(None), pl.ds(low * 128, (high - low) * 128))
        source, device = {
            PEER: (OWN, peer),
            ALONG: (OWN, along),
            RELAYED: (ALONG, ahead),
            PASSED: (ALONG + role, peer),
        }[target]
        sems = p_out.at[step, target, cut], p_in.at[step, target, cut]
        return send(buffer, at, source, target, *sems, device)

    def begin(step, buffer):
        for cut in range(cuts):
            block_copy(step, buffer, ALONG, cut).start()
            block_copy(step, buffer, PEER, cut).start()

    def relay(step, buffer, some):
        for cut in some:
            block_copy(step, buffer, ALONG, cut).wait_recv()

            @pl.when(has_ahead)
            def _():
                block_copy(step, buffer, RELAYED, cut).start()

            @pl.when(role == 0)
            def _():
                block_copy(step, buffer, PASSED, cut).start()

    def relay_again(step, buffer, some):
        @pl.when(has_behind)
        def _():
            for cut in some:
                block_copy(step, buffer, RELAYED, cut).wait_recv()

                @pl.when(role == 1)
                def _():
                    block_copy(step, buffer, PASSED, cut).start()

    every = range(cuts)
    load_start.wait()
    begin(0, starts)

    def receive_along(step):
        unit_copy(ALONG, step).wait_recv()

        @pl.when(has_ahead)
        def _():
            unit_copy(RELAYED, step).start()

        @pl.when(role == 0)
        def _():
            unit_copy(PASSED, step).start()

        unit_copy(PEER, step).wait_recv()
        piece(ALONG, step)
        piece(OWN, step)
        piece(PEER, step)

    def receive_relayed(step):
        unit_copy(RELAYED, step).wait_recv()

        @pl.when(role == 1)
        def _():
            unit_copy(PASSED, step).start()

        piece(RELAYED, step)

    def receive_passed(step):
        unit_copy(PASSED, step).wait_recv()
        piece(PASSED, step)

    def turn(step, carry):
        receive_along(step)
        pl.when((step >= 1) & has_behind)(lambda: receive_relayed(step - 1))
        pl.when((step >= 2) & has_passed)(lambda: receive_passed(step - 2))
        return carry

    lax.fori_loop(0, parts, turn, 0)
    half = cuts // 2
    relay(0, starts, every[:half])
    pl.when(has_behind)(lambda: receive_relayed(parts - 1))
    pl.when(has_passed)(lambda: receive_passed(parts - 2))
    relay(0, starts, every[half : cuts - 1])
    pl.when(has_passed)(lambda: receive_passed(parts - 1))

    for offset in range(1, W + 1):

        @pl.when(me >= offset)
        def _():
            keep_copy(offset).wait_recv()

    up_one, up_two = keep[0][0:1], keep[0][1:2]
    down_one, down_two = keep[1][0:1], keep[2][1:2]
    chosen = {
        PEER: jnp.where(core == 0, up_one, down_one),
        ALONG: jnp.where(side == 0, up_two, down_two),
        RELAYED: jnp.where(side == 0, down_two, up_two),
        PASSED: jnp.where(core == 0, down_one, up_one),
    }
    spread = {slot: jnp.concatenate([row] * (size // 128), axis=1) for slot, row in chosen.items()}
    columns = {slot: jnp.sum(sums[slot], axis=0, keepdims=True) for slot in range(5)}
    for slot, flag in spread.items():
        columns[slot] = flag * columns[slot]
    degrees = columns[OWN] + columns[PEER] + columns[ALONG] + columns[RELAYED] + columns[PASSED]
    degree_ref[...] = degrees
    each[OWN] = degrees

    def degree_copy(index, offset, slot):
        return pltpu.make_async_remote_copy(
            src_ref=each.at[OWN],
            dst_ref=each.at[slot],
            send_sem=d_out.at[index],
            recv_sem=d_in.at[slot],
            device_id={AXIS: me + offset},
            device_id_type=MESH,
        )

    notices = ((1, PEER + 3 * core), (-1, PASSED - 3 * core), (2, ALONG + side), (-2, RELAYED - side))
    for index, (offset, slot) in enumerate(notices):

        @pl.when((me + offset >= 0) & (me + offset < peers))
        def _():
            degree_copy(index, offset, slot).start()

    scale = lax.rsqrt(degrees)

    def product(buffer, slot):
        block = buffer[slot, :, :size]
        if slot != OWN:
            block = block * spread[slot].astype(jnp.bfloat16)
        value = lax.dot_general(block, tile[slot], ROWS_CONTRACTED, preferred_element_type=jnp.float32)
        if buffer.shape[2] > size:
            value = value + buffer[slot, :, size : size + 1].astype(jnp.float32) * columns[slot]
        return value

    def arrive(step, buffer, slot):
        for cut in every:
            block_copy(step, buffer, slot, cut).wait_recv()

    def scaled(slot):
        if slot != OWN:
            degree_copy(0, 0, slot).wait_recv()
        block = (starts[slot] * lax.rsqrt(each[slot])).astype(jnp.bfloat16)
        if slot != OWN:
            block = block * spread[slot].astype(jnp.bfloat16)
        return lax.dot_general(block, tile[slot], ROWS_CONTRACTED, preferred_element_type=jnp.float32)

    def gram_of(values):
        return lax.dot_general(
            values, values, LAST_CONTRACTED, precision=HIGH, preferred_element_type=jnp.float32
        )

    def phase_of(step, phase):
        return Phase(found[phase], box.at[step, phase], send_sem.at[step, phase], recv_sem.at[step, phase])

    def applied(inverse, values):
        return lax.dot_general(
            inverse, values, ROWS_CONTRACTED, precision=HIGH, preferred_element_type=jnp.float32
        )

    acc[...] = scaled(OWN)
    relay_again(0, starts, every[:1])
    relay(0, starts, every[cuts - 1 :])
    relay_again(0, starts, every[1:half])
    arrive(0, starts, PEER)
    acc[...] += scaled(PEER)
    acc[...] += scaled(ALONG)
    relay_again(0, starts, every[half:])

    @pl.when(has_behind)
    def _():
        acc[...] += scaled(RELAYED)

    @pl.when(has_passed)
    def _():
        arrive(0, starts, PASSED)
        acc[...] += scaled(PASSED)

    count = starts.shape[1]
    normed[...] = acc[...] * scale
    value = pack(gram_of(normed[...]))
    phases = [phase_of(0, phase) for phase in range(len(found))]
    phases[0].send(value)
    again = normed[...] * scale
    centre = jnp.sum(again, axis=1, keepdims=True) * (1.0 / size)
    centre = jnp.broadcast_to(centre, (count, 128)).astype(jnp.bfloat16)
    second[OWN, :, size:] = centre
    second[OWN, :, :size] = (again - centre[:, 0:1].astype(jnp.float32)).astype(jnp.bfloat16)
    begin(1, second)
    value = phases[0].receive()
    for phase in phases[1:]:
        phase.send(value)
        if phase is not phases[-1]:
            value = phase.receive()
    relay(1, second, every[:half])
    arrive(1, second, PEER)
    acc[...] = product(second, OWN) + product(second, PEER)
    relay(1, second, every[half:])
    value = phases[-1].receive()
    acc[...] += product(second, ALONG)
    quarter = count // 32
    inverse = inverse_factor(
        unpack(value),
        {
            quarter: lambda: relay_again(1, second, every[:half]),
            2 * quarter: lambda: relay_again(1, second, every[half:]),
        },
    )

    @pl.when(has_behind)
    def _():
        acc[...] += product(second, RELAYED)

    @pl.when(has_passed)
    def _():
        arrive(1, second, PASSED)
        acc[...] += product(second, PASSED)

    normed[...] = applied(inverse, acc[...] * scale)
    value = pack(gram_of(normed[...]))
    for phase in range(len(found)):
        now = phase_of(1, phase)
        now.send(value)
        value = now.receive()
        phases.append(now)
    out_ref[...] = applied(inverse_factor(unpack(value), {}), normed[...])
    for phase in phases:
        phase.settle()

    def settle(step, carry):
        unit_copy(ALONG, step).wait_send()
        unit_copy(PEER, step).wait_send()

        @pl.when(has_ahead)
        def _():
            unit_copy(RELAYED, step).wait_send()

        @pl.when((role == 0) | has_behind)
        def _():
            unit_copy(PASSED, step).wait_send()

        return carry

    lax.fori_loop(0, parts, settle, 0)
    for offset in range(1, W + 1):

        @pl.when(me + offset < peers)
        def _():
            keep_copy(offset).wait_send()

    for index, (offset, slot) in enumerate(notices):

        @pl.when((me + offset >= 0) & (me + offset < peers))
        def _():
            degree_copy(index, offset, slot).wait_send()

    for step, buffer in enumerate((starts, second)):
        for cut in range(cuts):
            block_copy(step, buffer, ALONG, cut).wait_send()
            block_copy(step, buffer, PEER, cut).wait_send()

            @pl.when(has_ahead)
            def _():
                block_copy(step, buffer, RELAYED, cut).wait_send()

            @pl.when((role == 0) | has_behind)
            def _():
                block_copy(step, buffer, PASSED, cut).wait_send()


def local(peers, features, iterate, band_mask):
    size, depth = features.shape
    count = iterate.shape[1]
    plan = radices(peers)
    phases, widest = len(plan), max(plan)
    parts, cuts = PARTS, CUTS
    dma = pltpu.SemaphoreType.DMA
    current, degrees = pl.pallas_call(
        functools.partial(fused_kernel, plan, peers, parts, cuts),
        out_shape=(
            jax.ShapeDtypeStruct((count, size), jnp.float32),
            jax.ShapeDtypeStruct((1, size), jnp.float32),
        ),
        in_specs=[pl.BlockSpec(memory_space=pltpu.HBM)] * 3,
        out_specs=(pl.BlockSpec(memory_space=pltpu.VMEM),) * 2,
        scratch_shapes=[
            pltpu.VMEM((size, depth), jnp.bfloat16),
            pltpu.VMEM((5, count, size), jnp.float32),
            pltpu.VMEM(band_mask.shape, jnp.int32),
            pltpu.VMEM((5, size, depth), jnp.bfloat16),
            pltpu.VMEM((depth, size), jnp.bfloat16),
            pltpu.VMEM((5, size, size), jnp.bfloat16),
            pltpu.VMEM((5, 8, size), jnp.float32),
            pltpu.VMEM((1 + W, 8, 128), jnp.float32),
            pltpu.VMEM((5, 1, size), jnp.float32),
            pltpu.VMEM((count, size), jnp.float32),
            pltpu.VMEM((count, size), jnp.float32),
            pltpu.VMEM((5, count, size + 128), jnp.bfloat16),
            pltpu.VMEM((ITERS, phases, widest, count // 2, 2 * count), jnp.float32),
            dma((3,)),
            dma((5, parts)),
            dma((5, parts)),
            dma((1 + W,)),
            dma((1 + W,)),
            dma((5,)),
            dma((5,)),
            dma((ITERS, 5, cuts)),
            dma((ITERS, 5, cuts)),
            dma((ITERS, phases, widest)),
            dma((ITERS, phases, widest)),
        ],
        compiler_params=pltpu.CompilerParams(
            collective_id=0, has_side_effects=True, vmem_limit_bytes=60 << 20
        ),
        name="fused",
    )(features, iterate.T, band_mask)
    return (current.T, degrees[0])


def solution(mesh):
    return jax.shard_map(
        functools.partial(local, mesh.shape[AXIS]),
        mesh=mesh,
        in_specs=(
            P(("groups", "rows"), None),
            P(("groups", "rows"), None),
            P(("groups", "rows"), None),
        ),
        out_specs=(P(("groups", "rows"), None), P(("groups", "rows"))),
        check_vma=False,
    )
```

```python
import functools

import jax
import jax.numpy as jnp
from jax import lax
from jax.experimental import pallas as pl
from jax.experimental.pallas import tpu as pltpu
from jax.sharding import PartitionSpec as P

W = 2
ITERS = 2
PARTS = 8
CUTS = 4
AXIS = "rows"
MESH = pl.DeviceIdType.MESH
HIGH = lax.Precision.HIGHEST


def radices(count):
    out = []
    while count > 1:
        radix = next((r for r in (4, 2, 3, 5, 7) if count % r == 0), count)
        out.append(radix)
        count //= radix
    return out


def peers_of(me, plan):
    stride = 1
    found = []
    for radix in plan:
        digit = lax.rem(lax.div(me, stride), radix)
        row = []
        for k in range(1, radix):
            other = lax.rem(digit + k, radix)
            row.append((other, me + (other - digit) * stride))
        found.append((digit, row))
        stride *= radix
    return found


class Phase:
    def __init__(self, found, box, send_sem, recv_sem):
        self.digit, self.row = found
        self.box, self.send_sem, self.recv_sem = box, send_sem, recv_sem

    def copy(self, k, slot, peer):
        return pltpu.make_async_remote_copy(
            src_ref=self.box.at[slot],
            dst_ref=self.box.at[slot],
            send_sem=self.send_sem.at[k],
            recv_sem=self.recv_sem.at[slot],
            device_id={AXIS: peer},
            device_id_type=MESH,
        )

    def send(self, value):
        self.box[self.digit] = value
        for k, (_, peer) in enumerate(self.row):
            self.copy(k, self.digit, peer).start()

    def receive(self):
        for k, (other, peer) in enumerate(self.row):
            self.copy(k, other, peer).wait_recv()
        value = self.box[0]
        for slot in range(1, len(self.row) + 1):
            value = value + self.box[slot]
        return value

    def settle(self):
        for k, (_, peer) in enumerate(self.row):
            self.copy(k, self.digit, peer).wait_send()


def inverse_factor(gram, pauses):
    size = gram.shape[0]
    rows = lax.broadcasted_iota(jnp.int32, (size, size), 0)
    cols = lax.broadcasted_iota(jnp.int32, (size, size), 1)
    both = jnp.concatenate([gram, jnp.where(rows == cols, 1.0, 0.0)], axis=1)
    count = size // 8
    bands = [both[8 * b : 8 * b + 8] for b in range(count)]
    sub = lax.broadcasted_iota(jnp.int32, (8, 2 * size), 0)
    out = []
    for b in range(count):
        if b in pauses:
            pauses[b]()
        panel = {
            c: [jnp.broadcast_to(bands[c][:, 8 * b + k : 8 * b + k + 1], (8, 2 * size)) for k in range(8)]
            for c in range(b, count)
        }
        diagonal = jnp.ones((8, 2 * size), jnp.float32)
        for k in range(8):
            pivot = panel[b][k][k : k + 1]
            inverse = 1.0 / pivot
            diagonal = jnp.where(sub == k, pivot, diagonal)
            row = bands[b][k : k + 1] * inverse
            heads = [panel[b][j][k : k + 1] * inverse for j in range(k + 1, 8)]
            for c in range(b, count):
                column = panel[c][k]
                if c == b:
                    column = jnp.where(sub > k, column, 0.0)
                bands[c] = bands[c] - column * row
                for j in range(k + 1, 8):
                    panel[c][j] = panel[c][j] - column * heads[j - k - 1]
        out.append((bands[b] * lax.rsqrt(diagonal))[:, size:])
    return jnp.concatenate(out, axis=0)


def pack(gram):
    half = gram.shape[0] // 2
    return jnp.concatenate([gram[:half], gram[half:]], axis=1)


def unpack(packed):
    size = packed.shape[1] // 2
    return jnp.concatenate([packed[:, :size], packed[:, size:]], axis=0)


OWN, PEER, ALONG, RELAYED, PASSED = range(5)
ROWS_CONTRACTED = (((1,), (0,)), ((), ()))
LAST_CONTRACTED = (((1,), (1,)), ((), ()))


def fused_kernel(plan, peers, parts, cuts, feature_hbm, start_hbm, mask_hbm, *refs):
    out_ref, degree_ref = refs[:2]
    feature_ref, starts, mask_ref, unit, flipped, tile, sums, keep, each, acc, normed, second, box = refs[2:15]
    loads, u_out, u_in, k_out, k_in, d_out, d_in, p_out, p_in, send_sem, recv_sem = refs[15:]
    load_feature = pltpu.make_async_copy(feature_hbm, feature_ref, loads.at[0])
    load_mask = pltpu.make_async_copy(mask_hbm, mask_ref, loads.at[1])
    load_start = pltpu.make_async_copy(start_hbm, starts.at[OWN], loads.at[2])
    load_feature.start()
    load_mask.start()
    load_start.start()
    me = lax.axis_index(AXIS)
    core = lax.rem(me, 2)
    side = lax.rem(lax.div(me, 2), 2)
    role = core + side - 2 * core * side
    peer = me + 1 - 2 * core
    along = me + 2 - 4 * side
    ahead = me + 4 - 8 * side
    behind = me - 4 + 8 * side
    has_ahead = (ahead >= 0) & (ahead < peers)
    has_behind = (behind >= 0) & (behind < peers)
    has_passed = (role == 1) | has_behind
    found = peers_of(me, plan)

    keep[1] = jnp.zeros((8, 128), jnp.float32)
    keep[2] = jnp.zeros((8, 128), jnp.float32)

    barrier = pltpu.get_barrier_semaphore()
    total = 0
    for _, row in found:
        for _, other in row:
            pl.semaphore_signal(barrier, inc=1, device_id={AXIS: other}, device_id_type=MESH)
            total += 1
    for offset in (1, 2, 4):

        @pl.when(me >= offset)
        def _():
            pl.semaphore_signal(barrier, inc=1, device_id={AXIS: me - offset}, device_id_type=MESH)

        @pl.when(me + offset < peers)
        def _():
            pl.semaphore_signal(barrier, inc=1, device_id={AXIS: me + offset}, device_id_type=MESH)

        total = total + (me >= offset).astype(jnp.int32) + (me + offset < peers).astype(jnp.int32)

    size = feature_ref.shape[0]
    width = size // parts
    sums[...] = jnp.zeros_like(sums)
    load_feature.wait()

    def normalise(step, carry):
        at = pl.ds(pl.multiple_of(step * width, width), width)
        values = feature_ref[at].astype(jnp.float32)
        square = jnp.sum(values * values, axis=-1, keepdims=True)
        unit[OWN, at] = (values * lax.rsqrt(square + 1e-06)).astype(jnp.bfloat16)
        return carry

    lax.fori_loop(0, parts, normalise, 0)
    pl.semaphore_wait(barrier, total)

    def send(buffer, at, source, target, out_sem, in_sem, device):
        return pltpu.make_async_remote_copy(
            src_ref=buffer.at[(source,) + at],
            dst_ref=buffer.at[(target,) + at],
            send_sem=out_sem,
            recv_sem=in_sem,
            device_id={AXIS: device},
            device_id_type=MESH,
        )

    def unit_copy(target, step):
        at = (pl.ds(pl.multiple_of(step * width, width), width),)
        source, device = {
            PEER: (OWN, peer),
            ALONG: (OWN, along),
            RELAYED: (ALONG, ahead),
            PASSED: (ALONG + role, peer),
        }[target]
        sems = u_out.at[target, step], u_in.at[target, step]
        return send(unit, at, source, target, *sems, device)

    def keep_copy(offset):
        return send(keep, (), 0, offset, k_out.at[offset], k_in.at[offset], me + offset)

    def launch(step, carry):
        unit_copy(ALONG, step).start()
        unit_copy(PEER, step).start()
        return carry

    lax.fori_loop(0, parts, launch, 0)
    load_mask.wait()
    row_at = lax.broadcasted_iota(jnp.int32, (8, 128), 0)
    flags = mask_ref[...].astype(jnp.float32)
    keep[0] = jnp.where(row_at == 0, flags[:, 0:1], jnp.where(row_at == 1, flags[:, 1:2], 0.0))
    flipped[...] = unit[OWN].T
    for offset in range(1, W + 1):

        @pl.when(me + offset < peers)
        def _():
            keep_copy(offset).start()

    def piece(slot, step):
        at = pl.ds(pl.multiple_of(step * width, width), width)
        scores = lax.dot_general(
            unit[slot, at], flipped[...], ROWS_CONTRACTED, preferred_element_type=jnp.float32
        )
        values = jnp.exp(scores).astype(jnp.bfloat16)
        tile[slot, at] = values
        sums[slot] += jnp.sum(values.astype(jnp.float32).reshape(width // 8, 8, size), axis=0)

    def block_copy(step, buffer, target, cut):
        units = buffer.shape[2] // 128
        low, high = -(-units * cut // cuts), -(-units * (cut + 1) // cuts)
        at = (slice(None), pl.ds(low * 128, (high - low) * 128))
        source, device = {
            PEER: (OWN, peer),
            ALONG: (OWN, along),
            RELAYED: (ALONG, ahead),
            PASSED: (ALONG + role, peer),
        }[target]
        sems = p_out.at[step, target, cut], p_in.at[step, target, cut]
        return send(buffer, at, source, target, *sems, device)

    def begin(step, buffer):
        for cut in range(cuts):
            block_copy(step, buffer, ALONG, cut).start()
            block_copy(step, buffer, PEER, cut).start()

    def relay(step, buffer, some):
        for cut in some:
            block_copy(step, buffer, ALONG, cut).wait_recv()

            @pl.when(has_ahead)
            def _():
                block_copy(step, buffer, RELAYED, cut).start()

            @pl.when(role == 0)
            def _():
                block_copy(step, buffer, PASSED, cut).start()

    def relay_again(step, buffer, some):
        @pl.when(has_behind)
        def _():
            for cut in some:
                block_copy(step, buffer, RELAYED, cut).wait_recv()

                @pl.when(role == 1)
                def _():
                    block_copy(step, buffer, PASSED, cut).start()

    every = range(cuts)
    load_start.wait()
    begin(0, starts)

    def receive_along(step):
        unit_copy(ALONG, step).wait_recv()

        @pl.when(has_ahead)
        def _():
            unit_copy(RELAYED, step).start()

        @pl.when(role == 0)
        def _():
            unit_copy(PASSED, step).start()

        unit_copy(PEER, step).wait_recv()
        piece(ALONG, step)
        piece(OWN, step)
        piece(PEER, step)

    def receive_relayed(step):
        unit_copy(RELAYED, step).wait_recv()

        @pl.when(role == 1)
        def _():
            unit_copy(PASSED, step).start()

        piece(RELAYED, step)

    def receive_passed(step):
        unit_copy(PASSED, step).wait_recv()
        piece(PASSED, step)

    def turn(step, carry):
        receive_along(step)
        pl.when((step >= 1) & has_behind)(lambda: receive_relayed(step - 1))
        pl.when((step >= 2) & has_passed)(lambda: receive_passed(step - 2))
        return carry

    lax.fori_loop(0, parts, turn, 0)
    half = cuts // 2
    relay(0, starts, every[:half])
    pl.when(has_behind)(lambda: receive_relayed(parts - 1))
    pl.when(has_passed)(lambda: receive_passed(parts - 2))
    relay(0, starts, every[half : cuts - 1])
    pl.when(has_passed)(lambda: receive_passed(parts - 1))

    for offset in range(1, W + 1):

        @pl.when(me >= offset)
        def _():
            keep_copy(offset).wait_recv()

    up_one, up_two = keep[0][0:1], keep[0][1:2]
    down_one, down_two = keep[1][0:1], keep[2][1:2]
    chosen = {
        PEER: jnp.where(core == 0, up_one, down_one),
        ALONG: jnp.where(side == 0, up_two, down_two),
        RELAYED: jnp.where(side == 0, down_two, up_two),
        PASSED: jnp.where(core == 0, down_one, up_one),
    }
    spread = {slot: jnp.concatenate([row] * (size // 128), axis=1) for slot, row in chosen.items()}
    columns = {slot: jnp.sum(sums[slot], axis=0, keepdims=True) for slot in range(5)}
    for slot, flag in spread.items():
        columns[slot] = flag * columns[slot]
    degrees = columns[OWN] + columns[PEER] + columns[ALONG] + columns[RELAYED] + columns[PASSED]
    degree_ref[...] = degrees
    each[OWN] = degrees

    def degree_copy(index, offset, slot):
        return pltpu.make_async_remote_copy(
            src_ref=each.at[OWN],
            dst_ref=each.at[slot],
            send_sem=d_out.at[index],
            recv_sem=d_in.at[slot],
            device_id={AXIS: me + offset},
            device_id_type=MESH,
        )

    notices = ((1, PEER + 3 * core), (-1, PASSED - 3 * core), (2, ALONG + side), (-2, RELAYED - side))
    for index, (offset, slot) in enumerate(notices):

        @pl.when((me + offset >= 0) & (me + offset < peers))
        def _():
            degree_copy(index, offset, slot).start()

    scale = lax.rsqrt(degrees)

    def product(buffer, slot):
        block = buffer[slot, :, :size]
        if slot != OWN:
            block = block * spread[slot].astype(jnp.bfloat16)
        value = lax.dot_general(block, tile[slot], ROWS_CONTRACTED, preferred_element_type=jnp.float32)
        if buffer.shape[2] > size:
            value = value + buffer[slot, :, size : size + 1].astype(jnp.float32) * columns[slot]
        return value

    def arrive(step, buffer, slot):
        for cut in every:
            block_copy(step, buffer, slot, cut).wait_recv()

    def scaled(slot):
        if slot != OWN:
            degree_copy(0, 0, slot).wait_recv()
        block = (starts[slot] * lax.rsqrt(each[slot])).astype(jnp.bfloat16)
        if slot != OWN:
            block = block * spread[slot].astype(jnp.bfloat16)
        return lax.dot_general(block, tile[slot], ROWS_CONTRACTED, preferred_element_type=jnp.float32)

    def gram_of(values):
        return lax.dot_general(
            values, values, LAST_CONTRACTED, precision=HIGH, preferred_element_type=jnp.float32
        )

    def phase_of(step, phase):
        return Phase(found[phase], box.at[step, phase], send_sem.at[step, phase], recv_sem.at[step, phase])

    def applied(inverse, values):
        return lax.dot_general(
            inverse, values, ROWS_CONTRACTED, precision=HIGH, preferred_element_type=jnp.float32
        )

    acc[...] = scaled(OWN)
    relay_again(0, starts, every[:1])
    relay(0, starts, every[cuts - 1 :])
    relay_again(0, starts, every[1:half])
    arrive(0, starts, PEER)
    acc[...] += scaled(PEER)
    acc[...] += scaled(ALONG)
    relay_again(0, starts, every[half:])

    @pl.when(has_behind)
    def _():
        acc[...] += scaled(RELAYED)

    @pl.when(has_passed)
    def _():
        arrive(0, starts, PASSED)
        acc[...] += scaled(PASSED)

    count = starts.shape[1]
    normed[...] = acc[...] * scale
    value = pack(gram_of(normed[...]))
    phases = [phase_of(0, phase) for phase in range(len(found))]
    phases[0].send(value)
    again = normed[...] * scale
    centre = jnp.sum(again, axis=1, keepdims=True) * (1.0 / size)
    centre = jnp.broadcast_to(centre, (count, 128)).astype(jnp.bfloat16)
    second[OWN, :, size:] = centre
    second[OWN, :, :size] = (again - centre[:, 0:1].astype(jnp.float32)).astype(jnp.bfloat16)
    begin(1, second)
    value = phases[0].receive()
    for phase in phases[1:]:
        phase.send(value)
        if phase is not phases[-1]:
            value = phase.receive()
    relay(1, second, every[:half])
    arrive(1, second, PEER)
    acc[...] = product(second, OWN) + product(second, PEER)
    relay(1, second, every[half:])
    value = phases[-1].receive()
    acc[...] += product(second, ALONG)
    quarter = count // 32
    inverse = inverse_factor(
        unpack(value),
        {
            quarter: lambda: relay_again(1, second, every[:half]),
            2 * quarter: lambda: relay_again(1, second, every[half:]),
        },
    )

    @pl.when(has_behind)
    def _():
        acc[...] += product(second, RELAYED)

    @pl.when(has_passed)
    def _():
        arrive(1, second, PASSED)
        acc[...] += product(second, PASSED)

    normed[...] = applied(inverse, acc[...] * scale)
    value = pack(gram_of(normed[...]))
    for phase in range(len(found)):
        now = phase_of(1, phase)
        now.send(value)
        value = now.receive()
        phases.append(now)
    out_ref[...] = applied(inverse_factor(unpack(value), {}), normed[...])
    for phase in phases:
        phase.settle()

    def settle(step, carry):
        unit_copy(ALONG, step).wait_send()
        unit_copy(PEER, step).wait_send()

        @pl.when(has_ahead)
        def _():
            unit_copy(RELAYED, step).wait_send()

        @pl.when((role == 0) | has_behind)
        def _():
            unit_copy(PASSED, step).wait_send()

        return carry

    lax.fori_loop(0, parts, settle, 0)
    for offset in range(1, W + 1):

        @pl.when(me + offset < peers)
        def _():
            keep_copy(offset).wait_send()

    for index, (offset, slot) in enumerate(notices):

        @pl.when((me + offset >= 0) & (me + offset < peers))
        def _():
            degree_copy(index, offset, slot).wait_send()

    for step, buffer in enumerate((starts, second)):
        for cut in range(cuts):
            block_copy(step, buffer, ALONG, cut).wait_send()
            block_copy(step, buffer, PEER, cut).wait_send()

            @pl.when(has_ahead)
            def _():
                block_copy(step, buffer, RELAYED, cut).wait_send()

            @pl.when((role == 0) | has_behind)
            def _():
                block_copy(step, buffer, PASSED, cut).wait_send()


def local(peers, features, iterate, band_mask):
    size, depth = features.shape
    count = iterate.shape[1]
    plan = radices(peers)
    phases, widest = len(plan), max(plan)
    parts, cuts = PARTS, CUTS
    dma = pltpu.SemaphoreType.DMA
    current, degrees = pl.pallas_call(
        functools.partial(fused_kernel, plan, peers, parts, cuts),
        out_shape=(
            jax.ShapeDtypeStruct((count, size), jnp.float32),
            jax.ShapeDtypeStruct((1, size), jnp.float32),
        ),
        in_specs=[pl.BlockSpec(memory_space=pltpu.HBM)] * 3,
        out_specs=(pl.BlockSpec(memory_space=pltpu.VMEM),) * 2,
        scratch_shapes=[
            pltpu.VMEM((size, depth), jnp.bfloat16),
            pltpu.VMEM((5, count, size), jnp.float32),
            pltpu.VMEM(band_mask.shape, jnp.int32),
            pltpu.VMEM((5, size, depth), jnp.bfloat16),
            pltpu.VMEM((depth, size), jnp.bfloat16),
            pltpu.VMEM((5, size, size), jnp.bfloat16),
            pltpu.VMEM((5, 8, size), jnp.float32),
            pltpu.VMEM((1 + W, 8, 128), jnp.float32),
            pltpu.VMEM((5, 1, size), jnp.float32),
            pltpu.VMEM((count, size), jnp.float32),
            pltpu.VMEM((count, size), jnp.float32),
            pltpu.VMEM((5, count, size + 128), jnp.bfloat16),
            pltpu.VMEM((ITERS, phases, widest, count // 2, 2 * count), jnp.float32),
            dma((3,)),
            dma((5, parts)),
            dma((5, parts)),
            dma((1 + W,)),
            dma((1 + W,)),
            dma((5,)),
            dma((5,)),
            dma((ITERS, 5, cuts)),
            dma((ITERS, 5, cuts)),
            dma((ITERS, phases, widest)),
            dma((ITERS, phases, widest)),
        ],
        compiler_params=pltpu.CompilerParams(
            collective_id=0, has_side_effects=True, vmem_limit_bytes=54848 << 10
        ),
        name="fused",
    )(features, iterate.T, band_mask)
    return (current.T, degrees[0])


def solution(mesh):
    return jax.shard_map(
        functools.partial(local, mesh.shape[AXIS]),
        mesh=mesh,
        in_specs=(
            P(("groups", "rows"), None),
            P(("groups", "rows"), None),
            P(("groups", "rows"), None),
        ),
        out_specs=(P(("groups", "rows"), None), P(("groups", "rows"))),
        check_vma=False,
    )
```

```python
import functools

import jax
import jax.numpy as jnp
from jax import lax
from jax.experimental import pallas as pl
from jax.experimental.pallas import tpu as pltpu
from jax.sharding import PartitionSpec as P

W = 2
ITERS = 2
PARTS = 8
CUTS = 4
AXIS = "rows"
MESH = pl.DeviceIdType.MESH
HIGH = lax.Precision.HIGHEST


def radices(count):
    out = []
    while count > 1:
        radix = next((r for r in (4, 2, 3, 5, 7) if count % r == 0), count)
        out.append(radix)
        count //= radix
    return out


def peers_of(me, plan):
    stride = 1
    found = []
    for radix in plan:
        digit = lax.rem(lax.div(me, stride), radix)
        row = []
        for k in range(1, radix):
            other = lax.rem(digit + k, radix)
            row.append((other, me + (other - digit) * stride))
        found.append((digit, row))
        stride *= radix
    return found


class Phase:
    def __init__(self, found, box, send_sem, recv_sem):
        self.digit, self.row = found
        self.box, self.send_sem, self.recv_sem = box, send_sem, recv_sem

    def copy(self, k, slot, peer):
        return pltpu.make_async_remote_copy(
            src_ref=self.box.at[slot],
            dst_ref=self.box.at[slot],
            send_sem=self.send_sem.at[k],
            recv_sem=self.recv_sem.at[slot],
            device_id={AXIS: peer},
            device_id_type=MESH,
        )

    def send(self, value):
        self.box[self.digit] = value
        for k, (_, peer) in enumerate(self.row):
            self.copy(k, self.digit, peer).start()

    def receive(self):
        for k, (other, peer) in enumerate(self.row):
            self.copy(k, other, peer).wait_recv()
        value = self.box[0]
        for slot in range(1, len(self.row) + 1):
            value = value + self.box[slot]
        return value

    def settle(self):
        for k, (_, peer) in enumerate(self.row):
            self.copy(k, self.digit, peer).wait_send()


def inverse_factor(gram, pauses):
    size = gram.shape[0]
    rows = lax.broadcasted_iota(jnp.int32, (size, size), 0)
    cols = lax.broadcasted_iota(jnp.int32, (size, size), 1)
    both = jnp.concatenate([gram, jnp.where(rows == cols, 1.0, 0.0)], axis=1)
    count = size // 8
    bands = [both[8 * b : 8 * b + 8] for b in range(count)]
    sub = lax.broadcasted_iota(jnp.int32, (8, 2 * size), 0)
    out = []
    for b in range(count):
        if b in pauses:
            pauses[b]()
        panel = {
            c: [jnp.broadcast_to(bands[c][:, 8 * b + k : 8 * b + k + 1], (8, 2 * size)) for k in range(8)]
            for c in range(b, count)
        }
        diagonal = jnp.ones((8, 2 * size), jnp.float32)
        for k in range(8):
            pivot = panel[b][k][k : k + 1]
            inverse = 1.0 / pivot
            diagonal = jnp.where(sub == k, pivot, diagonal)
            row = bands[b][k : k + 1] * inverse
            heads = [panel[b][j][k : k + 1] * inverse for j in range(k + 1, 8)]
            for c in range(b, count):
                column = panel[c][k]
                if c == b:
                    column = jnp.where(sub > k, column, 0.0)
                bands[c] = bands[c] - column * row
                for j in range(k + 1, 8):
                    panel[c][j] = panel[c][j] - column * heads[j - k - 1]
        out.append((bands[b] * lax.rsqrt(diagonal))[:, size:])
    return jnp.concatenate(out, axis=0)


def pack(gram):
    half = gram.shape[0] // 2
    return jnp.concatenate([gram[:half], gram[half:]], axis=1)


def unpack(packed):
    size = packed.shape[1] // 2
    return jnp.concatenate([packed[:, :size], packed[:, size:]], axis=0)


OWN, PEER, ALONG, RELAYED, PASSED = range(5)
ROWS_CONTRACTED = (((1,), (0,)), ((), ()))
LAST_CONTRACTED = (((1,), (1,)), ((), ()))


def fused_kernel(plan, peers, parts, cuts, feature_hbm, start_hbm, mask_hbm, *refs):
    out_ref, degree_ref = refs[:2]
    feature_ref, starts, mask_ref, unit, flipped, tile, sums, keep, each, acc, normed, second, box = refs[2:15]
    loads, u_out, u_in, k_out, k_in, d_out, d_in, p_out, p_in, send_sem, recv_sem = refs[15:]
    load_feature = pltpu.make_async_copy(feature_hbm, feature_ref, loads.at[0])
    load_mask = pltpu.make_async_copy(mask_hbm, mask_ref, loads.at[1])
    load_start = pltpu.make_async_copy(start_hbm, starts.at[OWN], loads.at[2])
    load_feature.start()
    load_mask.start()
    load_start.start()
    me = lax.axis_index(AXIS)
    core = lax.rem(me, 2)
    side = lax.rem(lax.div(me, 2), 2)
    role = core + side - 2 * core * side
    peer = me + 1 - 2 * core
    along = me + 2 - 4 * side
    ahead = me + 4 - 8 * side
    behind = me - 4 + 8 * side
    has_ahead = (ahead >= 0) & (ahead < peers)
    has_behind = (behind >= 0) & (behind < peers)
    has_passed = (role == 1) | has_behind
    found = peers_of(me, plan)

    keep[1] = jnp.zeros((8, 128), jnp.float32)
    keep[2] = jnp.zeros((8, 128), jnp.float32)

    barrier = pltpu.get_barrier_semaphore()
    total = 0
    for _, row in found[:1] + found[2:]:
        for _, other in row:
            pl.semaphore_signal(barrier, inc=1, device_id={AXIS: other}, device_id_type=MESH)
            total += 1
    for offset in (1, 2, 4):

        @pl.when(me >= offset)
        def _():
            pl.semaphore_signal(barrier, inc=1, device_id={AXIS: me - offset}, device_id_type=MESH)

        @pl.when(me + offset < peers)
        def _():
            pl.semaphore_signal(barrier, inc=1, device_id={AXIS: me + offset}, device_id_type=MESH)

        total = total + (me >= offset).astype(jnp.int32) + (me + offset < peers).astype(jnp.int32)

    size = feature_ref.shape[0]
    width = size // parts
    sums[...] = jnp.zeros_like(sums)
    load_feature.wait()

    def normalise(step, carry):
        at = pl.ds(pl.multiple_of(step * width, width), width)
        values = feature_ref[at].astype(jnp.float32)
        square = jnp.sum(values * values, axis=-1, keepdims=True)
        unit[OWN, at] = (values * lax.rsqrt(square + 1e-06)).astype(jnp.bfloat16)
        return carry

    lax.fori_loop(0, parts, normalise, 0)
    pl.semaphore_wait(barrier, total)

    def send(buffer, at, source, target, out_sem, in_sem, device):
        return pltpu.make_async_remote_copy(
            src_ref=buffer.at[(source,) + at],
            dst_ref=buffer.at[(target,) + at],
            send_sem=out_sem,
            recv_sem=in_sem,
            device_id={AXIS: device},
            device_id_type=MESH,
        )

    def unit_copy(target, step):
        at = (pl.ds(pl.multiple_of(step * width, width), width),)
        source, device = {
            PEER: (OWN, peer),
            ALONG: (OWN, along),
            RELAYED: (ALONG, ahead),
            PASSED: (ALONG + role, peer),
        }[target]
        sems = u_out.at[target, step], u_in.at[target, step]
        return send(unit, at, source, target, *sems, device)

    def keep_copy(offset):
        return send(keep, (), 0, offset, k_out.at[offset], k_in.at[offset], me + offset)

    def launch(step, carry):
        unit_copy(ALONG, step).start()
        unit_copy(PEER, step).start()
        return carry

    lax.fori_loop(0, parts, launch, 0)
    load_mask.wait()
    row_at = lax.broadcasted_iota(jnp.int32, (8, 128), 0)
    flags = mask_ref[...].astype(jnp.float32)
    keep[0] = jnp.where(row_at == 0, flags[:, 0:1], jnp.where(row_at == 1, flags[:, 1:2], 0.0))
    flipped[...] = unit[OWN].T
    for offset in range(1, W + 1):

        @pl.when(me + offset < peers)
        def _():
            keep_copy(offset).start()

    def piece(slot, step):
        at = pl.ds(pl.multiple_of(step * width, width), width)
        scores = lax.dot_general(
            unit[slot, at], flipped[...], ROWS_CONTRACTED, preferred_element_type=jnp.float32
        )
        values = jnp.exp(scores).astype(jnp.bfloat16)
        tile[slot, at] = values
        sums[slot] += jnp.sum(values.astype(jnp.float32).reshape(width // 8, 8, size), axis=0)

    def block_copy(step, buffer, target, cut):
        units = buffer.shape[2] // 128
        low, high = -(-units * cut // cuts), -(-units * (cut + 1) // cuts)
        at = (slice(None), pl.ds(low * 128, (high - low) * 128))
        source, device = {
            PEER: (OWN, peer),
            ALONG: (OWN, along),
            RELAYED: (ALONG, ahead),
            PASSED: (ALONG + role, peer),
        }[target]
        sems = p_out.at[step, target, cut], p_in.at[step, target, cut]
        return send(buffer, at, source, target, *sems, device)

    def begin(step, buffer):
        for cut in range(cuts):
            block_copy(step, buffer, ALONG, cut).start()
            block_copy(step, buffer, PEER, cut).start()

    def relay(step, buffer, some):
        for cut in some:
            block_copy(step, buffer, ALONG, cut).wait_recv()

            @pl.when(has_ahead)
            def _():
                block_copy(step, buffer, RELAYED, cut).start()

            @pl.when(role == 0)
            def _():
                block_copy(step, buffer, PASSED, cut).start()

    def relay_again(step, buffer, some):
        @pl.when(has_behind)
        def _():
            for cut in some:
                block_copy(step, buffer, RELAYED, cut).wait_recv()

                @pl.when(role == 1)
                def _():
                    block_copy(step, buffer, PASSED, cut).start()

    every = range(cuts)
    load_start.wait()
    begin(0, starts)

    def receive_along(step):
        unit_copy(ALONG, step).wait_recv()

        @pl.when(has_ahead)
        def _():
            unit_copy(RELAYED, step).start()

        @pl.when(role == 0)
        def _():
            unit_copy(PASSED, step).start()

        unit_copy(PEER, step).wait_recv()
        piece(ALONG, step)
        piece(PEER, step)

    def receive_relayed(step):
        unit_copy(RELAYED, step).wait_recv()

        @pl.when(role == 1)
        def _():
            unit_copy(PASSED, step).start()

        piece(RELAYED, step)

    def receive_passed(step):
        unit_copy(PASSED, step).wait_recv()
        piece(PASSED, step)

    def turn(step, carry):
        receive_along(step)
        pl.when((step >= 1) & has_behind)(lambda: receive_relayed(step - 1))
        pl.when((step >= 2) & has_passed)(lambda: receive_passed(step - 2))
        return carry

    def near(step, carry):
        piece(OWN, step)
        return carry

    lax.fori_loop(0, parts, near, 0)
    lax.fori_loop(0, parts, turn, 0)
    half = cuts // 2
    relay(0, starts, every[:half])
    pl.when(has_behind)(lambda: receive_relayed(parts - 1))
    pl.when(has_passed)(lambda: receive_passed(parts - 2))
    relay(0, starts, every[half : cuts - 1])
    pl.when(has_passed)(lambda: receive_passed(parts - 1))

    for offset in range(1, W + 1):

        @pl.when(me >= offset)
        def _():
            keep_copy(offset).wait_recv()

    up_one, up_two = keep[0][0:1], keep[0][1:2]
    down_one, down_two = keep[1][0:1], keep[2][1:2]
    chosen = {
        PEER: jnp.where(core == 0, up_one, down_one),
        ALONG: jnp.where(side == 0, up_two, down_two),
        RELAYED: jnp.where(side == 0, down_two, up_two),
        PASSED: jnp.where(core == 0, down_one, up_one),
    }
    spread = {slot: jnp.concatenate([row] * (size // 128), axis=1) for slot, row in chosen.items()}
    columns = {slot: jnp.sum(sums[slot], axis=0, keepdims=True) for slot in range(5)}
    for slot, flag in spread.items():
        columns[slot] = flag * columns[slot]
    degrees = columns[OWN] + columns[PEER] + columns[ALONG] + columns[RELAYED] + columns[PASSED]
    degree_ref[...] = degrees
    each[OWN] = degrees

    def degree_copy(index, offset, slot):
        return pltpu.make_async_remote_copy(
            src_ref=each.at[OWN],
            dst_ref=each.at[slot],
            send_sem=d_out.at[index],
            recv_sem=d_in.at[slot],
            device_id={AXIS: me + offset},
            device_id_type=MESH,
        )

    notices = ((1, PEER + 3 * core), (-1, PASSED - 3 * core), (2, ALONG + side), (-2, RELAYED - side))
    for index, (offset, slot) in enumerate(notices):

        @pl.when((me + offset >= 0) & (me + offset < peers))
        def _():
            degree_copy(index, offset, slot).start()

    scale = lax.rsqrt(degrees)

    def product(buffer, slot):
        block = buffer[slot, :, :size]
        if slot != OWN:
            block = block * spread[slot].astype(jnp.bfloat16)
        value = lax.dot_general(block, tile[slot], ROWS_CONTRACTED, preferred_element_type=jnp.float32)
        if buffer.shape[2] > size:
            value = value + buffer[slot, :, size : size + 1].astype(jnp.float32) * columns[slot]
        return value

    def arrive(step, buffer, slot):
        for cut in every:
            block_copy(step, buffer, slot, cut).wait_recv()

    def scaled(slot):
        if slot != OWN:
            degree_copy(0, 0, slot).wait_recv()
        block = (starts[slot] * lax.rsqrt(each[slot])).astype(jnp.bfloat16)
        if slot != OWN:
            block = block * spread[slot].astype(jnp.bfloat16)
        return lax.dot_general(block, tile[slot], ROWS_CONTRACTED, preferred_element_type=jnp.float32)

    def gram_of(values):
        return lax.dot_general(
            values, values, LAST_CONTRACTED, precision=HIGH, preferred_element_type=jnp.float32
        )

    def phase_of(step, phase):
        return Phase(found[phase], box.at[step, phase], send_sem.at[step, phase], recv_sem.at[step, phase])

    def applied(inverse, values):
        return lax.dot_general(
            inverse, values, ROWS_CONTRACTED, precision=HIGH, preferred_element_type=jnp.float32
        )

    acc[...] = scaled(OWN)
    relay_again(0, starts, every[:1])
    relay(0, starts, every[cuts - 1 :])
    relay_again(0, starts, every[1:half])
    arrive(0, starts, PEER)
    acc[...] += scaled(PEER)
    acc[...] += scaled(ALONG)
    relay_again(0, starts, every[half:])

    @pl.when(has_behind)
    def _():
        acc[...] += scaled(RELAYED)

    @pl.when(has_passed)
    def _():
        arrive(0, starts, PASSED)
        acc[...] += scaled(PASSED)

    count = starts.shape[1]
    normed[...] = acc[...] * scale
    value = pack(gram_of(normed[...]))
    phases = [phase_of(0, phase) for phase in range(len(found))]
    phases[0].send(value)
    again = normed[...] * scale
    centre = jnp.sum(again, axis=1, keepdims=True) * (1.0 / size)
    centre = jnp.broadcast_to(centre, (count, 128)).astype(jnp.bfloat16)
    second[OWN, :, size:] = centre
    second[OWN, :, :size] = (again - centre[:, 0:1].astype(jnp.float32)).astype(jnp.bfloat16)
    begin(1, second)
    value = phases[0].receive()
    for phase in phases[1:]:
        phase.send(value)
        if phase is not phases[-1]:
            value = phase.receive()
    relay(1, second, every[:half])
    arrive(1, second, PEER)
    acc[...] = product(second, OWN) + product(second, PEER)
    relay(1, second, every[half:])
    value = phases[-1].receive()
    acc[...] += product(second, ALONG)
    quarter = count // 32
    inverse = inverse_factor(
        unpack(value),
        {
            quarter: lambda: relay_again(1, second, every[:half]),
            2 * quarter: lambda: relay_again(1, second, every[half:]),
        },
    )

    @pl.when(has_behind)
    def _():
        acc[...] += product(second, RELAYED)

    @pl.when(has_passed)
    def _():
        arrive(1, second, PASSED)
        acc[...] += product(second, PASSED)

    normed[...] = applied(inverse, acc[...] * scale)
    value = pack(gram_of(normed[...]))
    for phase in range(len(found)):
        now = phase_of(1, phase)
        now.send(value)
        value = now.receive()
        phases.append(now)
    out_ref[...] = applied(inverse_factor(unpack(value), {}), normed[...])
    for phase in phases:
        phase.settle()

    def settle(step, carry):
        unit_copy(ALONG, step).wait_send()
        unit_copy(PEER, step).wait_send()

        @pl.when(has_ahead)
        def _():
            unit_copy(RELAYED, step).wait_send()

        @pl.when((role == 0) | has_behind)
        def _():
            unit_copy(PASSED, step).wait_send()

        return carry

    lax.fori_loop(0, parts, settle, 0)
    for offset in range(1, W + 1):

        @pl.when(me + offset < peers)
        def _():
            keep_copy(offset).wait_send()

    for index, (offset, slot) in enumerate(notices):

        @pl.when((me + offset >= 0) & (me + offset < peers))
        def _():
            degree_copy(index, offset, slot).wait_send()

    for step, buffer in enumerate((starts, second)):
        for cut in range(cuts):
            block_copy(step, buffer, ALONG, cut).wait_send()
            block_copy(step, buffer, PEER, cut).wait_send()

            @pl.when(has_ahead)
            def _():
                block_copy(step, buffer, RELAYED, cut).wait_send()

            @pl.when((role == 0) | has_behind)
            def _():
                block_copy(step, buffer, PASSED, cut).wait_send()


def local(peers, features, iterate, band_mask):
    size, depth = features.shape
    count = iterate.shape[1]
    plan = radices(peers)
    phases, widest = len(plan), max(plan)
    parts, cuts = PARTS, CUTS
    dma = pltpu.SemaphoreType.DMA
    current, degrees = pl.pallas_call(
        functools.partial(fused_kernel, plan, peers, parts, cuts),
        out_shape=(
            jax.ShapeDtypeStruct((count, size), jnp.float32),
            jax.ShapeDtypeStruct((1, size), jnp.float32),
        ),
        in_specs=[pl.BlockSpec(memory_space=pltpu.HBM)] * 3,
        out_specs=(pl.BlockSpec(memory_space=pltpu.VMEM),) * 2,
        scratch_shapes=[
            pltpu.VMEM((size, depth), jnp.bfloat16),
            pltpu.VMEM((5, count, size), jnp.float32),
            pltpu.VMEM(band_mask.shape, jnp.int32),
            pltpu.VMEM((5, size, depth), jnp.bfloat16),
            pltpu.VMEM((depth, size), jnp.bfloat16),
            pltpu.VMEM((5, size, size), jnp.bfloat16),
            pltpu.VMEM((5, 8, size), jnp.float32),
            pltpu.VMEM((1 + W, 8, 128), jnp.float32),
            pltpu.VMEM((5, 1, size), jnp.float32),
            pltpu.VMEM((count, size), jnp.float32),
            pltpu.VMEM((count, size), jnp.float32),
            pltpu.VMEM((5, count, size + 128), jnp.bfloat16),
            pltpu.VMEM((ITERS, phases, widest, count // 2, 2 * count), jnp.float32),
            dma((3,)),
            dma((5, parts)),
            dma((5, parts)),
            dma((1 + W,)),
            dma((1 + W,)),
            dma((5,)),
            dma((5,)),
            dma((ITERS, 5, cuts)),
            dma((ITERS, 5, cuts)),
            dma((ITERS, phases, widest)),
            dma((ITERS, phases, widest)),
        ],
        compiler_params=pltpu.CompilerParams(
            collective_id=0, has_side_effects=True, vmem_limit_bytes=54848 << 10
        ),
        name="fused",
    )(features, iterate.T, band_mask)
    return (current.T, degrees[0])


def solution(mesh):
    return jax.shard_map(
        functools.partial(local, mesh.shape[AXIS]),
        mesh=mesh,
        in_specs=(
            P(("groups", "rows"), None),
            P(("groups", "rows"), None),
            P(("groups", "rows"), None),
        ),
        out_specs=(P(("groups", "rows"), None), P(("groups", "rows"))),
        check_vma=False,
    )
```

```python
import functools

import jax
import jax.numpy as jnp
from jax import lax
from jax.experimental import pallas as pl
from jax.experimental.pallas import tpu as pltpu
from jax.sharding import PartitionSpec as P

W = 2
ITERS = 2
PARTS = 8
CUTS = 4
AXIS = "rows"
MESH = pl.DeviceIdType.MESH
HIGH = lax.Precision.HIGHEST


def radices(count):
    out = []
    while count > 1:
        radix = next((r for r in (4, 2, 3, 5, 7) if count % r == 0), count)
        out.append(radix)
        count //= radix
    return out


def peers_of(me, plan):
    stride = 1
    found = []
    for radix in plan:
        digit = lax.rem(lax.div(me, stride), radix)
        row = []
        for k in range(1, radix):
            other = lax.rem(digit + k, radix)
            row.append((other, me + (other - digit) * stride))
        found.append((digit, row))
        stride *= radix
    return found


class Phase:
    def __init__(self, found, box, send_sem, recv_sem):
        self.digit, self.row = found
        self.box, self.send_sem, self.recv_sem = box, send_sem, recv_sem

    def copy(self, k, slot, peer):
        return pltpu.make_async_remote_copy(
            src_ref=self.box.at[slot],
            dst_ref=self.box.at[slot],
            send_sem=self.send_sem.at[k],
            recv_sem=self.recv_sem.at[slot],
            device_id={AXIS: peer},
            device_id_type=MESH,
        )

    def send(self, value):
        self.box[self.digit] = value
        for k, (_, peer) in enumerate(self.row):
            self.copy(k, self.digit, peer).start()

    def receive(self):
        for k, (other, peer) in enumerate(self.row):
            self.copy(k, other, peer).wait_recv()
        value = self.box[0]
        for slot in range(1, len(self.row) + 1):
            value = value + self.box[slot]
        return value

    def settle(self):
        for k, (_, peer) in enumerate(self.row):
            self.copy(k, self.digit, peer).wait_send()


def inverse_factor(gram, pauses):
    size = gram.shape[0]
    rows = lax.broadcasted_iota(jnp.int32, (size, size), 0)
    cols = lax.broadcasted_iota(jnp.int32, (size, size), 1)
    both = jnp.concatenate([gram, jnp.where(rows == cols, 1.0, 0.0)], axis=1)
    count = size // 8
    bands = [both[8 * b : 8 * b + 8] for b in range(count)]
    sub = lax.broadcasted_iota(jnp.int32, (8, 2 * size), 0)
    out = []
    for b in range(count):
        if b in pauses:
            pauses[b]()
        panel = {
            c: [jnp.broadcast_to(bands[c][:, 8 * b + k : 8 * b + k + 1], (8, 2 * size)) for k in range(8)]
            for c in range(b, count)
        }
        diagonal = jnp.ones((8, 2 * size), jnp.float32)
        for k in range(8):
            pivot = panel[b][k][k : k + 1]
            inverse = 1.0 / pivot
            diagonal = jnp.where(sub == k, pivot, diagonal)
            row = bands[b][k : k + 1] * inverse
            heads = [panel[b][j][k : k + 1] * inverse for j in range(k + 1, 8)]
            for c in range(b, count):
                column = panel[c][k]
                if c == b:
                    column = jnp.where(sub > k, column, 0.0)
                bands[c] = bands[c] - column * row
                for j in range(k + 1, 8):
                    panel[c][j] = panel[c][j] - column * heads[j - k - 1]
        out.append((bands[b] * lax.rsqrt(diagonal))[:, size:])
    return jnp.concatenate(out, axis=0)


def pack(gram):
    half = gram.shape[0] // 2
    return jnp.concatenate([gram[:half], gram[half:]], axis=1)


def unpack(packed):
    size = packed.shape[1] // 2
    return jnp.concatenate([packed[:, :size], packed[:, size:]], axis=0)


OWN, PEER, ALONG, RELAYED, PASSED = range(5)
ROWS_CONTRACTED = (((1,), (0,)), ((), ()))
LAST_CONTRACTED = (((1,), (1,)), ((), ()))


def fused_kernel(plan, peers, parts, cuts, feature_hbm, start_hbm, mask_hbm, *refs):
    out_ref, degree_ref = refs[:2]
    feature_ref, starts, mask_ref, unit, flipped, tile, sums, keep, each, acc, normed, second, box = refs[2:15]
    loads, u_out, u_in, k_out, k_in, d_out, d_in, p_out, p_in, send_sem, recv_sem = refs[15:]
    middle = feature_ref.shape[0] // 2
    load_feature = [
        pltpu.make_async_copy(
            feature_hbm.at[pl.ds(at * middle, middle)], feature_ref.at[pl.ds(at * middle, middle)], loads.at[2 * at]
        )
        for at in range(2)
    ]
    load_mask = pltpu.make_async_copy(mask_hbm, mask_ref, loads.at[1])
    load_start = pltpu.make_async_copy(start_hbm, starts.at[OWN], loads.at[3])
    load_feature[0].start()
    load_feature[1].start()
    load_mask.start()
    load_start.start()
    me = lax.axis_index(AXIS)
    core = lax.rem(me, 2)
    side = lax.rem(lax.div(me, 2), 2)
    role = core + side - 2 * core * side
    peer = me + 1 - 2 * core
    along = me + 2 - 4 * side
    ahead = me + 4 - 8 * side
    behind = me - 4 + 8 * side
    has_ahead = (ahead >= 0) & (ahead < peers)
    has_behind = (behind >= 0) & (behind < peers)
    has_passed = (role == 1) | has_behind
    found = peers_of(me, plan)

    keep[1] = jnp.zeros((8, 128), jnp.float32)
    keep[2] = jnp.zeros((8, 128), jnp.float32)

    barrier = pltpu.get_barrier_semaphore()
    total = 0
    for _, row in found[:1] + found[2:]:
        for _, other in row:
            pl.semaphore_signal(barrier, inc=1, device_id={AXIS: other}, device_id_type=MESH)
            total += 1
    for offset in (1, 2, 4):

        @pl.when(me >= offset)
        def _():
            pl.semaphore_signal(barrier, inc=1, device_id={AXIS: me - offset}, device_id_type=MESH)

        @pl.when(me + offset < peers)
        def _():
            pl.semaphore_signal(barrier, inc=1, device_id={AXIS: me + offset}, device_id_type=MESH)

        total = total + (me >= offset).astype(jnp.int32) + (me + offset < peers).astype(jnp.int32)

    size = feature_ref.shape[0]
    width = size // parts
    sums[...] = jnp.zeros_like(sums)
    load_feature[0].wait()

    def normalise(step, carry):
        at = pl.ds(pl.multiple_of(step * width, width), width)
        values = feature_ref[at].astype(jnp.float32)
        square = jnp.sum(values * values, axis=-1, keepdims=True)
        unit[OWN, at] = (values * lax.rsqrt(square + 1e-06)).astype(jnp.bfloat16)
        return carry

    lax.fori_loop(0, parts // 2, normalise, 0)
    load_feature[1].wait()
    lax.fori_loop(parts // 2, parts, normalise, 0)
    pl.semaphore_wait(barrier, total)

    def send(buffer, at, source, target, out_sem, in_sem, device):
        return pltpu.make_async_remote_copy(
            src_ref=buffer.at[(source,) + at],
            dst_ref=buffer.at[(target,) + at],
            send_sem=out_sem,
            recv_sem=in_sem,
            device_id={AXIS: device},
            device_id_type=MESH,
        )

    def unit_copy(target, step):
        at = (pl.ds(pl.multiple_of(step * width, width), width),)
        source, device = {
            PEER: (OWN, peer),
            ALONG: (OWN, along),
            RELAYED: (ALONG, ahead),
            PASSED: (ALONG + role, peer),
        }[target]
        sems = u_out.at[target, step], u_in.at[target, step]
        return send(unit, at, source, target, *sems, device)

    def keep_copy(offset):
        return send(keep, (), 0, offset, k_out.at[offset], k_in.at[offset], me + offset)

    def launch(step, carry):
        unit_copy(ALONG, step).start()
        unit_copy(PEER, step).start()
        return carry

    lax.fori_loop(0, parts, launch, 0)
    load_mask.wait()
    row_at = lax.broadcasted_iota(jnp.int32, (8, 128), 0)
    flags = mask_ref[...].astype(jnp.float32)
    keep[0] = jnp.where(row_at == 0, flags[:, 0:1], jnp.where(row_at == 1, flags[:, 1:2], 0.0))
    flipped[...] = unit[OWN].T
    for offset in range(1, W + 1):

        @pl.when(me + offset < peers)
        def _():
            keep_copy(offset).start()

    def piece(slot, step):
        at = pl.ds(pl.multiple_of(step * width, width), width)
        scores = lax.dot_general(
            unit[slot, at], flipped[...], ROWS_CONTRACTED, preferred_element_type=jnp.float32
        )
        values = jnp.exp(scores).astype(jnp.bfloat16)
        tile[slot, at] = values
        sums[slot] += jnp.sum(values.astype(jnp.float32).reshape(width // 8, 8, size), axis=0)

    def block_copy(step, buffer, target, cut):
        units = buffer.shape[2] // 128
        low, high = -(-units * cut // cuts), -(-units * (cut + 1) // cuts)
        at = (slice(None), pl.ds(low * 128, (high - low) * 128))
        source, device = {
            PEER: (OWN, peer),
            ALONG: (OWN, along),
            RELAYED: (ALONG, ahead),
            PASSED: (ALONG + role, peer),
        }[target]
        sems = p_out.at[step, target, cut], p_in.at[step, target, cut]
        return send(buffer, at, source, target, *sems, device)

    def begin(step, buffer):
        for cut in range(cuts):
            block_copy(step, buffer, ALONG, cut).start()
            block_copy(step, buffer, PEER, cut).start()

    def relay(step, buffer, some):
        for cut in some:
            block_copy(step, buffer, ALONG, cut).wait_recv()

            @pl.when(has_ahead)
            def _():
                block_copy(step, buffer, RELAYED, cut).start()

            @pl.when(role == 0)
            def _():
                block_copy(step, buffer, PASSED, cut).start()

    def relay_again(step, buffer, some):
        @pl.when(has_behind)
        def _():
            for cut in some:
                block_copy(step, buffer, RELAYED, cut).wait_recv()

                @pl.when(role == 1)
                def _():
                    block_copy(step, buffer, PASSED, cut).start()

    every = range(cuts)
    load_start.wait()
    begin(0, starts)

    def receive_along(step):
        unit_copy(ALONG, step).wait_recv()

        @pl.when(has_ahead)
        def _():
            unit_copy(RELAYED, step).start()

        @pl.when(role == 0)
        def _():
            unit_copy(PASSED, step).start()

        unit_copy(PEER, step).wait_recv()
        piece(ALONG, step)
        piece(PEER, step)

    def receive_relayed(step):
        unit_copy(RELAYED, step).wait_recv()

        @pl.when(role == 1)
        def _():
            unit_copy(PASSED, step).start()

        piece(RELAYED, step)

    def receive_passed(step):
        unit_copy(PASSED, step).wait_recv()
        piece(PASSED, step)

    def turn(step, carry):
        receive_along(step)
        pl.when((step >= 1) & has_behind)(lambda: receive_relayed(step - 1))
        pl.when((step >= 2) & has_passed)(lambda: receive_passed(step - 2))
        return carry

    def near(step, carry):
        piece(OWN, step)
        return carry

    lax.fori_loop(0, parts, near, 0)
    lax.fori_loop(0, parts, turn, 0)
    half = cuts // 2
    relay(0, starts, every[:half])
    pl.when(has_behind)(lambda: receive_relayed(parts - 1))
    pl.when(has_passed)(lambda: receive_passed(parts - 2))
    relay(0, starts, every[half : cuts - 1])
    pl.when(has_passed)(lambda: receive_passed(parts - 1))

    for offset in range(1, W + 1):

        @pl.when(me >= offset)
        def _():
            keep_copy(offset).wait_recv()

    up_one, up_two = keep[0][0:1], keep[0][1:2]
    down_one, down_two = keep[1][0:1], keep[2][1:2]
    chosen = {
        PEER: jnp.where(core == 0, up_one, down_one),
        ALONG: jnp.where(side == 0, up_two, down_two),
        RELAYED: jnp.where(side == 0, down_two, up_two),
        PASSED: jnp.where(core == 0, down_one, up_one),
    }
    spread = {slot: jnp.concatenate([row] * (size // 128), axis=1) for slot, row in chosen.items()}
    columns = {slot: jnp.sum(sums[slot], axis=0, keepdims=True) for slot in range(5)}
    for slot, flag in spread.items():
        columns[slot] = flag * columns[slot]
    degrees = columns[OWN] + columns[PEER] + columns[ALONG] + columns[RELAYED] + columns[PASSED]
    degree_ref[...] = degrees
    each[OWN] = degrees

    def degree_copy(index, offset, slot):
        return pltpu.make_async_remote_copy(
            src_ref=each.at[OWN],
            dst_ref=each.at[slot],
            send_sem=d_out.at[index],
            recv_sem=d_in.at[slot],
            device_id={AXIS: me + offset},
            device_id_type=MESH,
        )

    notices = ((1, PEER + 3 * core), (-1, PASSED - 3 * core), (2, ALONG + side), (-2, RELAYED - side))
    for index, (offset, slot) in enumerate(notices):

        @pl.when((me + offset >= 0) & (me + offset < peers))
        def _():
            degree_copy(index, offset, slot).start()

    scale = lax.rsqrt(degrees)

    def product(buffer, slot):
        block = buffer[slot, :, :size]
        if slot != OWN:
            block = block * spread[slot].astype(jnp.bfloat16)
        value = lax.dot_general(block, tile[slot], ROWS_CONTRACTED, preferred_element_type=jnp.float32)
        if buffer.shape[2] > size:
            value = value + buffer[slot, :, size : size + 1].astype(jnp.float32) * columns[slot]
        return value

    def arrive(step, buffer, slot):
        for cut in every:
            block_copy(step, buffer, slot, cut).wait_recv()

    def scaled(slot):
        if slot != OWN:
            degree_copy(0, 0, slot).wait_recv()
        block = (starts[slot] * lax.rsqrt(each[slot])).astype(jnp.bfloat16)
        if slot != OWN:
            block = block * spread[slot].astype(jnp.bfloat16)
        return lax.dot_general(block, tile[slot], ROWS_CONTRACTED, preferred_element_type=jnp.float32)

    def gram_of(values):
        return lax.dot_general(
            values, values, LAST_CONTRACTED, precision=HIGH, preferred_element_type=jnp.float32
        )

    def phase_of(step, phase):
        return Phase(found[phase], box.at[step, phase], send_sem.at[step, phase], recv_sem.at[step, phase])

    def applied(inverse, values):
        return lax.dot_general(
            inverse, values, ROWS_CONTRACTED, precision=HIGH, preferred_element_type=jnp.float32
        )

    acc[...] = scaled(OWN)
    relay_again(0, starts, every[:1])
    relay(0, starts, every[cuts - 1 :])
    relay_again(0, starts, every[1:half])
    arrive(0, starts, PEER)
    acc[...] += scaled(PEER)
    acc[...] += scaled(ALONG)
    relay_again(0, starts, every[half:])

    @pl.when(has_behind)
    def _():
        acc[...] += scaled(RELAYED)

    @pl.when(has_passed)
    def _():
        arrive(0, starts, PASSED)
        acc[...] += scaled(PASSED)

    count = starts.shape[1]
    normed[...] = acc[...] * scale
    value = pack(gram_of(normed[...]))
    phases = [phase_of(0, phase) for phase in range(len(found))]
    phases[0].send(value)
    again = normed[...] * scale
    centre = jnp.sum(again, axis=1, keepdims=True) * (1.0 / size)
    centre = jnp.broadcast_to(centre, (count, 128)).astype(jnp.bfloat16)
    second[OWN, :, size:] = centre
    second[OWN, :, :size] = (again - centre[:, 0:1].astype(jnp.float32)).astype(jnp.bfloat16)
    begin(1, second)
    value = phases[0].receive()
    for phase in phases[1:]:
        phase.send(value)
        if phase is not phases[-1]:
            value = phase.receive()
    relay(1, second, every[:half])
    arrive(1, second, PEER)
    acc[...] = product(second, OWN) + product(second, PEER)
    relay(1, second, every[half:])
    value = phases[-1].receive()
    acc[...] += product(second, ALONG)
    quarter = count // 32
    inverse = inverse_factor(
        unpack(value),
        {
            quarter: lambda: relay_again(1, second, every[:half]),
            2 * quarter: lambda: relay_again(1, second, every[half:]),
        },
    )

    @pl.when(has_behind)
    def _():
        acc[...] += product(second, RELAYED)

    @pl.when(has_passed)
    def _():
        arrive(1, second, PASSED)
        acc[...] += product(second, PASSED)

    normed[...] = applied(inverse, acc[...] * scale)
    value = pack(gram_of(normed[...]))
    for phase in range(len(found)):
        now = phase_of(1, phase)
        now.send(value)
        value = now.receive()
        phases.append(now)
    out_ref[...] = applied(inverse_factor(unpack(value), {}), normed[...])
    for phase in phases:
        phase.settle()

    def settle(step, carry):
        unit_copy(ALONG, step).wait_send()
        unit_copy(PEER, step).wait_send()

        @pl.when(has_ahead)
        def _():
            unit_copy(RELAYED, step).wait_send()

        @pl.when((role == 0) | has_behind)
        def _():
            unit_copy(PASSED, step).wait_send()

        return carry

    lax.fori_loop(0, parts, settle, 0)
    for offset in range(1, W + 1):

        @pl.when(me + offset < peers)
        def _():
            keep_copy(offset).wait_send()

    for index, (offset, slot) in enumerate(notices):

        @pl.when((me + offset >= 0) & (me + offset < peers))
        def _():
            degree_copy(index, offset, slot).wait_send()

    for step, buffer in enumerate((starts, second)):
        for cut in range(cuts):
            block_copy(step, buffer, ALONG, cut).wait_send()
            block_copy(step, buffer, PEER, cut).wait_send()

            @pl.when(has_ahead)
            def _():
                block_copy(step, buffer, RELAYED, cut).wait_send()

            @pl.when((role == 0) | has_behind)
            def _():
                block_copy(step, buffer, PASSED, cut).wait_send()


def local(peers, features, iterate, band_mask):
    size, depth = features.shape
    count = iterate.shape[1]
    plan = radices(peers)
    phases, widest = len(plan), max(plan)
    parts, cuts = PARTS, CUTS
    dma = pltpu.SemaphoreType.DMA
    current, degrees = pl.pallas_call(
        functools.partial(fused_kernel, plan, peers, parts, cuts),
        out_shape=(
            jax.ShapeDtypeStruct((count, size), jnp.float32),
            jax.ShapeDtypeStruct((1, size), jnp.float32),
        ),
        in_specs=[pl.BlockSpec(memory_space=pltpu.HBM)] * 3,
        out_specs=(pl.BlockSpec(memory_space=pltpu.VMEM),) * 2,
        scratch_shapes=[
            pltpu.VMEM((size, depth), jnp.bfloat16),
            pltpu.VMEM((5, count, size), jnp.float32),
            pltpu.VMEM(band_mask.shape, jnp.int32),
            pltpu.VMEM((5, size, depth), jnp.bfloat16),
            pltpu.VMEM((depth, size), jnp.bfloat16),
            pltpu.VMEM((5, size, size), jnp.bfloat16),
            pltpu.VMEM((5, 8, size), jnp.float32),
            pltpu.VMEM((1 + W, 8, 128), jnp.float32),
            pltpu.VMEM((5, 1, size), jnp.float32),
            pltpu.VMEM((count, size), jnp.float32),
            pltpu.VMEM((count, size), jnp.float32),
            pltpu.VMEM((5, count, size + 128), jnp.bfloat16),
            pltpu.VMEM((ITERS, phases, widest, count // 2, 2 * count), jnp.float32),
            dma((4,)),
            dma((5, parts)),
            dma((5, parts)),
            dma((1 + W,)),
            dma((1 + W,)),
            dma((5,)),
            dma((5,)),
            dma((ITERS, 5, cuts)),
            dma((ITERS, 5, cuts)),
            dma((ITERS, phases, widest)),
            dma((ITERS, phases, widest)),
        ],
        compiler_params=pltpu.CompilerParams(
            collective_id=0, has_side_effects=True, vmem_limit_bytes=54848 << 10
        ),
        name="fused",
    )(features, iterate.T, band_mask)
    return (current.T, degrees[0])


def solution(mesh):
    return jax.shard_map(
        functools.partial(local, mesh.shape[AXIS]),
        mesh=mesh,
        in_specs=(
            P(("groups", "rows"), None),
            P(("groups", "rows"), None),
            P(("groups", "rows"), None),
        ),
        out_specs=(P(("groups", "rows"), None), P(("groups", "rows"))),
        check_vma=False,
    )
```
